512 devices in a mesh: blk: 64 (over x, y, z_hi), uly: 8 (over z_lo, core).
Axes of the slice: x: 4, y: 8, z: 8 (z_hi: 2, z_lo: 4; z = z_hi * 4 + z_lo), core: 2. Of those that a mesh axis runs over, the one named last changes fastest.
Arguments:
- residual: bfloat16 [6144, 2048], P(('blk', 'uly')), may hold values from -24 to 24
- query_projection: bfloat16 [6144, 4096], P(('blk', 'uly')), may hold values from -51 to 51
- key_projection: bfloat16 [6144, 1024], P(('blk', 'uly')), may hold values from -5.1 to 5.1
- value_projection: bfloat16 [6144, 1024], P(('blk', 'uly')), may hold values from -6 to 6
- gate_proj: bfloat16 [6144, 4096], P(('blk', 'uly')), may hold values from -6 to 6
- positions: int32 [6144], replicated, may hold values from 0 to 6143, each once
- prefix_len: int32 [1], replicated, may hold values from 768 to 3071
- out_weight: bfloat16 [4096, 2048], P('uly', 'blk'), may hold values from -0.375 to 0.375
- norm_gain: float32 [2048], replicated, may hold values from 0.1 to 1.9
- gate_weight: bfloat16 [2048, 6144], P('blk', 'uly'), may hold values from -0.125 to 0.125
- up_weight: bfloat16 [2048, 6144], P('blk', 'uly'), may hold values from -0.125 to 0.125
- down_weight: bfloat16 [6144, 2048], P('uly', 'blk'), may hold values from -0.078125 to 0.078125
Outputs:
- layer_out: bfloat16 [6144, 2048], P(('blk', 'uly'))
The draws below stay inside these ranges and needn't reach their ends.
Inputs may be any that keep to these rules, and one draw needn't show every extreme that they name: `positions`: each of 0 to 6143 appears once.
All inputs are finite; a program needn't handle non-finite values.
Results may differ from the reference program's by a relative error of at most 0.014.
Values may be sent and summed in bfloat16 or wider, within the bound.
A program may use at most 64 MiB of HBM per device.

```python
import math
import jax
import jax.numpy as jnp
from jax import lax

D = 2048
QUERY_HEAD_COUNT = 32
KEY_VALUE_HEADS = 8
HEAD_SIZE = 128
FF = 6144
TOK_DEV = 12
SEQUENCE_TOKENS = 6144
N_ULY = 8


def attention_parts(key):
    base_key = jax.random.fold_in(key, 4242)
    random_key_sample, query_draw = jax.random.split(base_key, 2)
    key_row_set = jnp.clip(jax.random.normal(random_key_sample, (SEQUENCE_TOKENS, KEY_VALUE_HEADS * HEAD_SIZE), jnp.float32), -3.0, 3.0) * 1.6
    query_rows = jnp.clip(jax.random.normal(query_draw, (SEQUENCE_TOKENS, QUERY_HEAD_COUNT * HEAD_SIZE), jnp.float32), -3.0, 3.0) * 1.6
    return (query_rows, key_row_set)


def draw_query_projection(key, part):
    return attention_parts(key)[0].astype(jnp.bfloat16)


def draw_key_projection(key, part):
    return attention_parts(key)[1].astype(jnp.bfloat16)


def draw_residual(key, part):
    base_key = jax.random.fold_in(key, 515)
    noise_key, row_key, col_key = jax.random.split(base_key, 3)
    row_scale = jnp.exp(jax.random.uniform(row_key, (SEQUENCE_TOKENS, 1), jnp.float32, math.log(0.2), math.log(2.0)))
    col_scale = jnp.exp(jax.random.uniform(col_key, (1, D), jnp.float32, math.log(0.3), math.log(3.0)))
    noise = jnp.clip(jax.random.normal(noise_key, (SEQUENCE_TOKENS, D), jnp.float32), -4.0, 4.0)
    return (noise * row_scale * col_scale).astype(jnp.bfloat16)


def block_levels(stream_key, dims, shards, least, high):
    def one(axis_at, parts):
        draws = jax.random.uniform(jax.random.fold_in(jax.random.fold_in(stream_key, 6), axis_at), (parts,), jnp.float32, least / len(shards), high / len(shards))
        return jnp.repeat(jnp.exp(draws), dims[axis_at] // parts).reshape((-1,) + (1,) * (len(dims) - axis_at - 1))

    level = one(*shards[0])
    for cut in shards[1:]:
        level = level * one(*cut)
    return level


def normal_values(stream_key, shape, scale, bound, cuts=(), dtype=jnp.bfloat16):
    result = scale * jax.random.normal(stream_key, shape, jnp.float32)
    if cuts:
        result = result * block_levels(stream_key, shape, cuts, -0.22, 0.18)
    return jnp.clip(result, -bound, bound).astype(dtype)


def setup_inputs(seed: int = 0) -> dict:
    arg_keys = jax.random.split(jax.random.key(seed), 13)
    return {
        "residual": draw_residual(jax.random.fold_in(arg_keys[12], 71), 0),
        "query_projection": draw_query_projection(jax.random.fold_in(arg_keys[12], 71), 0),
        "key_projection": draw_key_projection(jax.random.fold_in(arg_keys[12], 71), 0),
        "value_projection": normal_values(arg_keys[3], (SEQUENCE_TOKENS, KEY_VALUE_HEADS * HEAD_SIZE), 1.0, 6.0, ((0, 512),)),
        "gate_proj": normal_values(arg_keys[4], (SEQUENCE_TOKENS, QUERY_HEAD_COUNT * HEAD_SIZE), 1.5, 6.0, ((0, 512),)),
        "positions": jax.random.permutation(arg_keys[5], SEQUENCE_TOKENS).astype(jnp.int32),
        "prefix_len": jax.random.randint(arg_keys[6], (1,), SEQUENCE_TOKENS // 8, SEQUENCE_TOKENS // 2).astype(jnp.int32),
        "out_weight": normal_values(arg_keys[7], (QUERY_HEAD_COUNT * HEAD_SIZE, D), (QUERY_HEAD_COUNT * HEAD_SIZE // 16) ** -0.5, 0.375, ((0, 8), (1, 64))),
        "norm_gain": jnp.clip(1.0 + 0.18 * jax.random.normal(arg_keys[8], (D,), jnp.float32), 0.1, 1.9),
        "gate_weight": normal_values(arg_keys[9], (D, FF), D ** -0.5, 0.125, ((0, 64), (1, 8))),
        "up_weight": normal_values(arg_keys[10], (D, FF), D ** -0.5, 0.125, ((0, 64), (1, 8))),
        "down_weight": normal_values(arg_keys[11], (FF, D), FF ** -0.5, 0.078125, ((0, 8), (1, 64))),
    }


def rounded_parts(left, right, groups):
    width = left.shape[1] // groups
    total = jnp.zeros((left.shape[0], right.shape[1]), jnp.float32)
    for group in range(groups):
        piece = jnp.dot(left[:, group * width:(group + 1) * width], right[group * width:(group + 1) * width, :], preferred_element_type=jnp.float32)
        total = total + lax.optimization_barrier(piece.astype(jnp.bfloat16)).astype(jnp.float32)
    return total

def reference(residual, query_projection, key_projection, value_projection, gate_proj, positions, prefix_len, out_weight, norm_gain, gate_weight, up_weight, down_weight):
    heads_per_group = QUERY_HEAD_COUNT // KEY_VALUE_HEADS
    score_scale = 1.0 / math.sqrt(HEAD_SIZE)
    rows_per_block = TOK_DEV * N_ULY
    count_of_blocks = SEQUENCE_TOKENS // rows_per_block
    gathered_keys = key_projection.astype(jnp.float32).reshape(SEQUENCE_TOKENS, KEY_VALUE_HEADS, HEAD_SIZE)
    gathered_values = value_projection.astype(jnp.float32).reshape(SEQUENCE_TOKENS, KEY_VALUE_HEADS, HEAD_SIZE)
    prefix = prefix_len[0]
    query_block_list = query_projection.reshape(count_of_blocks, rows_per_block, KEY_VALUE_HEADS, heads_per_group, HEAD_SIZE)
    pos_blocks = positions.reshape(count_of_blocks, rows_per_block)

    def attend_block(pieces):
        query_part, query_pos = pieces
        scores = jnp.einsum('bkgd,skd->bkgs', query_part.astype(jnp.float32), gathered_keys) * score_scale
        visible = (positions[None, :] <= query_pos[:, None]) | (positions[None, :] < prefix)
        scores = jnp.where(visible[:, None, None, :], scores, -jnp.inf)
        row_max = lax.optimization_barrier(jnp.max(scores, axis=-1, keepdims=True))
        exp_scores = jnp.exp(scores - row_max)
        denom = lax.optimization_barrier(jnp.sum(exp_scores, axis=-1))
        probs = lax.optimization_barrier(exp_scores.astype(jnp.bfloat16)).astype(jnp.float32)
        summed = jnp.einsum('bkgs,skd->bkgd', probs, gathered_values)
        return (summed / denom[..., None]).reshape(rows_per_block, QUERY_HEAD_COUNT * HEAD_SIZE)
    attended = lax.map(attend_block, (query_block_list, pos_blocks)).reshape(SEQUENCE_TOKENS, QUERY_HEAD_COUNT * HEAD_SIZE)
    gated_out = (attended * jax.nn.sigmoid(gate_proj.astype(jnp.float32))).astype(jnp.bfloat16)
    projected = rounded_parts(gated_out, out_weight, N_ULY)
    hidden_sum = (residual.astype(jnp.float32) + projected).astype(jnp.bfloat16)
    hidden_f = hidden_sum.astype(jnp.float32)
    mean_sq = lax.optimization_barrier(jnp.mean(hidden_f * hidden_f, axis=-1, keepdims=True))
    normed = (hidden_f * lax.rsqrt(mean_sq + 1e-06) * norm_gain.astype(jnp.float32)).astype(jnp.bfloat16)
    gate_sum = jnp.dot(normed, gate_weight, preferred_element_type=jnp.float32)
    up_sum = jnp.dot(normed, up_weight, preferred_element_type=jnp.float32)
    activated = (jax.nn.silu(gate_sum) * up_sum).astype(jnp.bfloat16)
    ffn_out = rounded_parts(activated, down_weight, N_ULY)
    return (hidden_f + ffn_out).astype(jnp.bfloat16)
```

```python
import functools
import math

import jax
import jax.numpy as jnp
from jax import lax
from jax.experimental import pallas as pl
from jax.experimental.pallas import tpu as pltpu
from jax.sharding import PartitionSpec as P

MESH = pl.DeviceIdType.MESH
HEAD_SIZE = 128
GROUP = 4
NX, NY = 4, 8
TOK = 12
PAD = 16
D = 2048
FFC = 768
CHUNK = 768
F32 = jnp.float32
BF16 = jnp.bfloat16
NEG = -1e30


def remote(src, dst, ss, rs, dest):
    return pltpu.make_async_remote_copy(
        src_ref=src, dst_ref=dst, send_sem=ss, recv_sem=rs, device_id=dest, device_id_type=MESH
    )


class Ring:
    def __init__(self, get, half, me, n, to, ss, rs):
        self.get, self.half, self.me, self.n, self.to, self.ss, self.rs = get, half, me, n, to, ss, rs
        self.sent = []

    def pos(self, d):
        return lax.rem(self.me + (d + self.n), self.n)

    def send(self, ref, way, t):
        step = 1 if way == 0 else -1
        cp = remote(ref, ref, self.ss.at[way, t], self.rs.at[way, t], self.to(self.pos(step)))
        cp.start()
        self.sent.append(cp)

    def wait(self, ref, way, t):
        remote(ref, ref, self.ss.at[way, t], self.rs.at[way, t], self.to(self.pos(1))).wait_recv()

    def start(self):
        own = self.get(self.me)
        self.send(own, 0, 0)
        self.send(own, 1, 0)

    def step(self, t):
        h = self.n // 2
        for way in (0, 1):
            j = self.pos(-t if way == 0 else t)
            self.wait(self.get(j), way, t - 1)
            self.send(self.get(j) if t < h - 1 else self.half(j, way), way, t)

    def finish(self):
        h = self.n // 2
        j = self.pos(h)
        for way in (0, 1):
            self.wait(self.half(j, way), way, h - 1)


def kernel(
    q_ref, k_ref, v_ref, g_ref, res_ref, tq_ref, posk_ref, gain_ref, wo_ref, wg_ref, wu_ref, wd_ref,
    out_ref,
    q16, k16, v16, g16, krec, vrec, qrec, grec, cmp_buf,
    bufk, bufv, bufo, bufg, bufu, bufd,
    m_sc, l_sc, acc, gated, pbuf, rbuf, hid, nrm, nbuf, act,
    a_ss, a_rs, w_ss, w_rs, x_ss, x_rs, y_ss, y_rs, c_ss, c_rs, r_ss, r_rs, n_ss, n_rs, f_ss, f_rs,
):
    blk, uly = lax.axis_index("blk"), lax.axis_index("uly")
    x, y, zh = lax.div(blk, 16), lax.rem(lax.div(blk, 2), 8), lax.rem(blk, 2)
    zl, c = lax.div(uly, 2), lax.rem(uly, 2)
    z = zh * 4 + zl

    def dev(x_, y_, zh_, zl_, c_):
        return ((x_ * NY + y_) * 2 + zh_, zl_ * 2 + c_)

    home = zh == c

    q16[0:TOK, :] = q_ref[...]
    k16[0:TOK, :] = k_ref[...]
    v16[0:TOK, :] = v_ref[...]
    g16[0:TOK, :] = g_ref[...]

    def out_peer(d):
        z2 = lax.rem(z + d, 8)
        zh2, zl2 = lax.div(z2, 4), lax.rem(z2, 4)
        return dev(x, y, zh2, zl2, zh), zl2 * 2 + zh2

    def in_peer(d):
        s = lax.rem(uly + d, 8)
        return dev(x, y, c, lax.div(s, 2), lax.rem(s, 2)), s

    other = dev(x, y, zh, zl, 1 - c)
    xto = lambda p: dev(p, y, zh, zl, c)
    yto = lambda p: dev(x, p, zh, zl, c)

    barrier = pltpu.get_barrier_semaphore()

    def greet(dest):
        pl.semaphore_signal(barrier, inc=1, device_id=dest, device_id_type=MESH)

    for d in (1, NX - 1):
        greet(xto(lax.rem(x + d, NX)))
    for d in (1, NY - 1):
        greet(yto(lax.rem(y + d, NY)))
    greet(other)
    for d in range(8):
        def both(d=d):
            greet(out_peer(d)[0])
            greet(in_peer(d)[0])
        if d == 0:
            pl.when(jnp.logical_not(home))(both)
        else:
            both()
    pl.when(home)(lambda: pl.semaphore_wait(barrier, 19))
    pl.when(jnp.logical_not(home))(lambda: pl.semaphore_wait(barrier, 21))

    order = (4, 3, 5, 2, 6, 1, 7, 0)

    def spread(src, dst, ss, rs):
        def make(d):
            dest, head = out_peer(d)
            return src(head), dst.at[uly], ss.at[d], rs.at[uly], dest
        return make

    def collect(src, dst, ss, rs):
        def make(d):
            dest, slot = in_peer(d)
            return src(slot), dst.at[zl * 2 + zh], ss.at[d], rs.at[zl * 2 + zh], dest
        return make

    def send_all(make):
        for d in order:
            s, t, a, b, dest = make(d)
            if d == 0:
                pl.when(home)(lambda s=s, t=t, b=b: pltpu.make_async_copy(s, t, b).start())
                pl.when(jnp.logical_not(home))(lambda s=s, t=t, a=a, b=b, dest=dest: remote(s, t, a, b, dest).start())
            else:
                remote(s, t, a, b, dest).start()

    def wait_all_sent(make):
        for d in order:
            s, t, a, b, dest = make(d)
            if d == 0:
                pl.when(jnp.logical_not(home))(lambda s=s, t=t, a=a, b=b, dest=dest: remote(s, t, a, b, dest).wait_send())
            else:
                remote(s, t, a, b, dest).wait_send()

    def wait_all_recv(dst, ss, rs):
        for i in range(8):
            remote(dst.at[i], dst.at[i], ss.at[i], rs.at[i], other).wait_recv()

    def cols(ref, width):
        return lambda head: ref.at[:, pl.ds(pl.multiple_of(head * width, 128), width)]

    moves = [
        spread(cols(k16, HEAD_SIZE), krec, a_ss.at[0], a_rs.at[0]),
        spread(cols(v16, HEAD_SIZE), vrec, a_ss.at[1], a_rs.at[1]),
        spread(cols(q16, GROUP * HEAD_SIZE), qrec, a_ss.at[2], a_rs.at[2]),
        spread(cols(g16, GROUP * HEAD_SIZE), grec, a_ss.at[3], a_rs.at[3]),
    ]
    send_all(moves[0])
    send_all(moves[1])

    weights = [(wo_ref, bufo), (wg_ref, bufg), (wu_ref, bufu), (wd_ref, bufd)]
    twin = dev(x, y, c, zl, zh)

    def swap(i):
        src, buf = weights[i]
        return src, buf.at[x, y, zh], w_ss.at[i], w_rs.at[i], twin

    def swap_start():
        for i in range(4):
            s, t, a, b, dest = swap(i)
            pl.when(home)(lambda s=s, t=t, b=b: pltpu.make_async_copy(s, t, b).start())
            pl.when(jnp.logical_not(home))(lambda s=s, t=t, a=a, b=b, dest=dest: remote(s, t, a, b, dest).start())

    def swap_wait(i):
        own = weights[i][1].at[x, y, c]
        remote(own, own, w_ss.at[i], w_rs.at[i], other).wait_recv()

    swap_start()
    send_all(moves[2])
    send_all(moves[3])

    sent = []

    def gather(buf, idx, x_first, rows):
        rx = dict(n=NX, me=x, to=xto, ss=x_ss.at[idx], rs=x_rs.at[idx])
        ry = dict(n=NY, me=y, to=yto, ss=y_ss.at[idx], rs=y_rs.at[idx])
        hr = rows // 2
        if x_first:
            one = Ring(lambda i: buf.at[i, y, c], lambda i, w: buf.at[i, y, c, pl.ds(w * hr, hr)], **rx)
            two = Ring(lambda i: buf.at[:, i, c], lambda i, w: buf.at[pl.ds(w * 2, 2), i, c], **ry)
            theirs = lambda i: buf.at[:, i, 1 - c]
        else:
            one = Ring(lambda i: buf.at[x, i, c], lambda i, w: buf.at[x, i, c, pl.ds(w * hr, hr)], **ry)
            two = Ring(lambda i: buf.at[i, :, c], lambda i, w: buf.at[i, pl.ds(w * 4, 4), c], **rx)
            theirs = lambda i: buf.at[i, :, 1 - c]

        def give(j, t):
            cp = remote(two.get(j), two.get(j), c_ss.at[idx, t], c_rs.at[idx, t], other)
            cp.start()
            sent.append(cp)

        one.start()
        yield
        for t in range(1, one.n // 2):
            one.step(t)
            yield
        one.finish()
        yield
        two.start()
        give(two.me, 0)
        yield
        for t in range(1, two.n // 2):
            two.step(t)
            give(two.pos(-t), 2 * t - 1)
            give(two.pos(t), 2 * t)
            yield
        two.finish()
        give(two.pos(two.n // 2), two.n - 1)
        yield
        for t in range(two.n):
            d = 0 if t == 0 else (-(t + 1) // 2 if t % 2 else t // 2)
            if t == two.n - 1:
                d = two.n // 2
            ref = theirs(two.pos(d))
            remote(ref, ref, c_ss.at[idx, t], c_rs.at[idx, t], other).wait_recv()
        sent.extend(one.sent + two.sent)
        yield

    def compact(rec, buf):
        for s in range(8):
            cmp_buf[TOK * s:TOK * (s + 1), :] = rec[s].astype(F32)[:TOK]
        buf[x, y, c] = cmp_buf[...].astype(BF16)

    gk = gather(bufk, 0, True, 96)
    gv = gather(bufv, 1, False, 96)
    go = gather(bufo, 2, True, 32)
    gg = gather(bufg, 3, True, 32)
    gu = gather(bufu, 4, False, 32)
    gd = gather(bufd, 5, False, 32)

    def run(gens, times):
        for _ in range(times):
            for gen in gens:
                next(gen, None)

    wait_all_recv(krec, a_ss.at[0], a_rs.at[0])
    compact(krec, bufk)
    next(gk)
    wait_all_recv(vrec, a_ss.at[1], a_rs.at[1])
    compact(vrec, bufv)
    next(gv)
    for i in range(4):
        swap_wait(i)
    run([gk, gv, go, gg, gu, gd], 2)
    run([gk, gv], 2)
    run([gk, gv, go, gg, gu, gd], 1)
    run([gk, gv], 2)
    run([gu, gd], 2)
    run([go, gg, gu, gd], 1)
    run([gk, gv], 9)
    wait_all_recv(qrec, a_ss.at[2], a_rs.at[2])
    wait_all_recv(grec, a_ss.at[3], a_rs.at[3])

    m_sc[...] = jnp.full_like(m_sc, NEG)
    l_sc[...] = jnp.zeros_like(l_sc)
    acc[...] = jnp.zeros_like(acc)
    scale = 1.0 / math.sqrt(HEAD_SIZE)

    def attend(i, _):
        xi, yi = lax.div(i, 2), lax.rem(i, 2) * 4
        keys = bufk[xi, pl.ds(yi, 4)].reshape(CHUNK, HEAD_SIZE)
        vals = bufv[xi, pl.ds(yi, 4)].reshape(CHUNK, HEAD_SIZE)
        visible = posk_ref[i] <= tq_ref[...]
        for g in range(GROUP):
            q = qrec[:, :, g * HEAD_SIZE:(g + 1) * HEAD_SIZE].reshape(8 * PAD, HEAD_SIZE)
            s = lax.dot_general(q, keys, (((1,), (1,)), ((), ())), preferred_element_type=F32) * scale
            s = jnp.where(visible, s, NEG)
            old = m_sc[g]
            new = jnp.maximum(old, jnp.max(s, axis=1, keepdims=True))
            p = jnp.exp(s - new)
            f = jnp.exp(old - new)
            l_sc[g] = l_sc[g] * f + jnp.sum(p, axis=1, keepdims=True)
            acc[g] = acc[g] * f + jnp.dot(p.astype(BF16), vals, preferred_element_type=F32)
            m_sc[g] = new
        return 0

    lax.fori_loop(0, 8, attend, 0)
    for g in range(GROUP):
        gate = grec[:, :, g * HEAD_SIZE:(g + 1) * HEAD_SIZE].reshape(8 * PAD, HEAD_SIZE).astype(F32)
        gated[:, g * HEAD_SIZE:(g + 1) * HEAD_SIZE] = (acc[g] / l_sc[g] * jax.nn.sigmoid(gate)).astype(BF16)

    run([go, gg, gu, gd], 9)

    NT = (((1,), (1,)), ((), ()))

    def project(lhs, buf, width):
        def body(i, _):
            w = buf[i].reshape(512, width)
            part = lax.dot_general(lhs, w, NT, preferred_element_type=F32).astype(BF16)
            pbuf[:, :, pl.ds(pl.multiple_of(i * 512, 128), 512)] = part.reshape(8, PAD, 512)
            return 0
        lax.fori_loop(0, NX, body, 0)

    block = lambda s: pbuf.at[s]

    def total():
        t = rbuf[0].astype(F32)
        for i in range(1, 8):
            t = t + rbuf[i].astype(F32)
        return t

    project(gated[...], bufo, 512)
    first = collect(block, rbuf, r_ss, r_rs)
    send_all(first)
    wait_all_recv(rbuf, r_ss, r_rs)
    hid[0:TOK, :] = (res_ref[...].astype(F32) + total()[:TOK]).astype(BF16)
    hf = hid[...].astype(F32)
    mean_sq = jnp.mean(hf * hf, axis=-1, keepdims=True)
    nrm[...] = (hf * lax.rsqrt(mean_sq + 1e-06) * gain_ref[...]).astype(BF16)
    normed = spread(lambda head: nrm, nbuf, n_ss, n_rs)
    send_all(normed)
    wait_all_recv(nbuf, n_ss, n_rs)

    rows = nbuf[...].reshape(8 * PAD, D)
    for n in range(FFC // 256):
        at = slice(n * 256, (n + 1) * 256)
        gate_sum = jnp.zeros((8 * PAD, 256), F32)
        up_sum = jnp.zeros((8 * PAD, 256), F32)
        for i in range(NX):
            r = rows[:, i * 512:(i + 1) * 512]
            gate_sum += jnp.dot(r, bufg[i, :, :, :, at].reshape(512, 256), preferred_element_type=F32)
            up_sum += jnp.dot(r, bufu[i, :, :, :, at].reshape(512, 256), preferred_element_type=F32)
        act[:, at] = (jax.nn.silu(gate_sum) * up_sum).astype(BF16)

    wait_all_sent(first)
    project(act[...], bufd, FFC)
    last = collect(block, rbuf, f_ss, f_rs)
    send_all(last)
    wait_all_recv(rbuf, f_ss, f_rs)
    out_ref[...] = (hid[...].astype(F32) + total())[:TOK].astype(BF16)

    wait_all_sent(last)
    wait_all_sent(normed)
    for m in moves:
        wait_all_sent(m)
    for i in range(4):
        s, t, a, b, dest = swap(i)
        pl.when(jnp.logical_not(home))(lambda s=s, t=t, a=a, b=b, dest=dest: remote(s, t, a, b, dest).wait_send())
    for cp in sent:
        cp.wait_send()


def per_device(
    residual, query_projection, key_projection, value_projection, gate_proj, positions, prefix_len,
    out_weight, norm_gain, gate_weight, up_weight, down_weight,
):
    blk, uly = lax.axis_index("blk"), lax.axis_index("uly")
    first = (blk // 2 * 2 + uly % 2) * 96
    mine = lax.dynamic_slice_in_dim(positions, first, 96).reshape(8, TOK)
    tq = jnp.maximum(jnp.pad(mine, ((0, 0), (0, PAD - TOK))), prefix_len[0] - 1).reshape(8 * PAD, 1)
    posk = positions.reshape(8, 1, CHUNK)
    vm = pl.BlockSpec(memory_space=pltpu.VMEM)
    dma = pltpu.SemaphoreType.DMA
    half = lambda r, w: pltpu.VMEM((NX, NY, 2, r, w), BF16)
    return pl.pallas_call(
        kernel,
        out_shape=jax.ShapeDtypeStruct((TOK, D), BF16),
        in_specs=[vm] * 12,
        out_specs=vm,
        scratch_shapes=[
            pltpu.VMEM((PAD, 4096), BF16),
            pltpu.VMEM((PAD, 1024), BF16),
            pltpu.VMEM((PAD, 1024), BF16),
            pltpu.VMEM((PAD, 4096), BF16),
            pltpu.VMEM((8, PAD, 128), BF16),
            pltpu.VMEM((8, PAD, 128), BF16),
            pltpu.VMEM((8, PAD, 512), BF16),
            pltpu.VMEM((8, PAD, 512), BF16),
            pltpu.VMEM((96, 128), F32),
            half(96, 128), half(96, 128), half(32, 512), half(32, FFC), half(32, FFC), half(32, FFC),
            pltpu.VMEM((GROUP, 8 * PAD, 1), F32),
            pltpu.VMEM((GROUP, 8 * PAD, 1), F32),
            pltpu.VMEM((GROUP, 8 * PAD, HEAD_SIZE), F32),
            pltpu.VMEM((8 * PAD, GROUP * HEAD_SIZE), BF16),
            pltpu.VMEM((8, PAD, D), BF16),
            pltpu.VMEM((8, PAD, D), BF16),
            pltpu.VMEM((PAD, D), BF16),
            pltpu.VMEM((PAD, D), BF16),
            pltpu.VMEM((8, PAD, D), BF16),
            pltpu.VMEM((8 * PAD, FFC), BF16),
            dma((4, 8)), dma((4, 8)),
            dma((4,)), dma((4,)),
            dma((6, 2, 2)), dma((6, 2, 2)),
            dma((6, 2, 4)), dma((6, 2, 4)),
            dma((6, 8)), dma((6, 8)),
            dma((8,)), dma((8,)),
            dma((8,)), dma((8,)),
            dma((8,)), dma((8,)),
        ],
        compiler_params=pltpu.CompilerParams(
            collective_id=0, has_side_effects=True, vmem_limit_bytes=60 * 2**20
        ),
        name="layer",
    )(
        query_projection, key_projection, value_projection, gate_proj, residual, tq, posk,
        norm_gain.reshape(1, D), out_weight.T, gate_weight, up_weight, down_weight.T,
    )


def solution(mesh):
    return jax.shard_map(
        per_device,
        mesh=mesh,
        in_specs=(
            P(("blk", "uly"), None),
            P(("blk", "uly"), None),
            P(("blk", "uly"), None),
            P(("blk", "uly"), None),
            P(("blk", "uly"), None),
            P(),
            P(),
            P("uly", "blk"),
            P(),
            P("blk", "uly"),
            P("blk", "uly"),
            P("uly", "blk"),
        ),
        out_specs=P(("blk", "uly"), None),
        check_vma=False,
    )
```

```python
import functools
import math

import jax
import jax.numpy as jnp
from jax import lax
from jax.experimental import pallas as pl
from jax.experimental.pallas import tpu as pltpu
from jax.sharding import PartitionSpec as P

MESH = pl.DeviceIdType.MESH
HEAD_SIZE = 128
GROUP = 4
NX, NY = 4, 8
TOK = 12
PAD = 16
D = 2048
FFC = 768
CHUNK = 768
F32 = jnp.float32
BF16 = jnp.bfloat16
NEG = -1e30
STAGE = 99


def remote(src, dst, ss, rs, dest):
    return pltpu.make_async_remote_copy(
        src_ref=src, dst_ref=dst, send_sem=ss, recv_sem=rs, device_id=dest, device_id_type=MESH
    )


class Ring:
    def __init__(self, get, half, me, n, to, ss, rs, log):
        self.get, self.half, self.me, self.n, self.to, self.ss, self.rs = get, half, me, n, to, ss, rs
        self.sent = log

    def pos(self, d):
        return lax.rem(self.me + (d + self.n), self.n)

    def send(self, ref, way, t):
        step = 1 if way == 0 else -1
        cp = remote(ref, ref, self.ss.at[way, t], self.rs.at[way, t], self.to(self.pos(step)))
        cp.start()
        self.sent.append(cp)

    def wait(self, ref, way, t):
        remote(ref, ref, self.ss.at[way, t], self.rs.at[way, t], self.to(self.pos(1))).wait_recv()

    def start(self):
        own = self.get(self.me)
        self.send(own, 0, 0)
        self.send(own, 1, 0)

    def step(self, t):
        h = self.n // 2
        for way in (0, 1):
            j = self.pos(-t if way == 0 else t)
            self.wait(self.get(j), way, t - 1)
            self.send(self.get(j) if t < h - 1 else self.half(j, way), way, t)

    def finish(self):
        h = self.n // 2
        j = self.pos(h)
        for way in (0, 1):
            self.wait(self.half(j, way), way, h - 1)


class Direct:
    def __init__(self, get, me, n, to, ss, rs, log):
        self.get, self.me, self.n, self.to, self.ss, self.rs, self.sent = get, me, n, to, ss, rs, log

    def pos(self, d):
        return lax.rem(self.me + d, self.n)

    def start(self):
        own = self.get(self.me)
        for d in range(1, self.n):
            cp = remote(own, own, self.ss.at[d // 2, d % 2], self.rs.at[d // 2, d % 2], self.to(self.pos(d)))
            cp.start()
            self.sent.append(cp)

    def finish(self):
        for d in range(1, self.n):
            ref = self.get(self.pos(self.n - d))
            remote(ref, ref, self.ss.at[d // 2, d % 2], self.rs.at[d // 2, d % 2], self.to(self.pos(1))).wait_recv()


def pack(v):
    lo, hi = v[:, :8], v[:, 8:]
    turn = lambda t: jnp.concatenate([t[:, 4:], t[:, :4]], axis=1)
    extra = jnp.concatenate([turn(lo[..., 384:]), lo[..., 384:], turn(hi[..., 384:])], axis=2)
    row = lax.broadcasted_iota(jnp.int32, extra.shape, 1)
    return jnp.concatenate([lo[..., :384], jnp.where(row < 4, hi[..., :384], extra)], axis=1)


def unpack(v):
    lo, hi = v[:, :8], v[:, 8:]
    turn = lambda t: jnp.concatenate([t[:, 4:], t[:, :4]], axis=1)
    a, b, d = hi[..., :128], hi[..., 128:256], hi[..., 256:]
    row = lax.broadcasted_iota(jnp.int32, a.shape, 1)
    last = jnp.concatenate([jnp.where(row < 4, turn(a), b), turn(d)], axis=1)
    return jnp.concatenate([v, last], axis=2)


def kernel(
    q_ref, k_ref, v_ref, g_ref, res_ref, tq_ref, posk_ref, gain_ref, wo_ref, wg_ref, wu_ref, wd_ref,
    out_ref,
    q16, k16, v16, g16, krec, vrec, qrec, grec, cmp_buf,
    bufk, bufv, bufo, bufg, bufu, bufd,
    m_sc, l_sc, acc, gated, pbuf, rbuf, sbuf, fbuf, hid, nrm, nbuf, rows, act,
    a_ss, a_rs, w_ss, w_rs, x_ss, x_rs, y_ss, y_rs, c_ss, c_rs, r_ss, r_rs, n_ss, n_rs, f_ss, f_rs,
):
    blk, uly = lax.axis_index("blk"), lax.axis_index("uly")
    x, y, zh = lax.div(blk, 16), lax.rem(lax.div(blk, 2), 8), lax.rem(blk, 2)
    zl, c = lax.div(uly, 2), lax.rem(uly, 2)
    z = zh * 4 + zl

    def dev(x_, y_, zh_, zl_, c_):
        return ((x_ * NY + y_) * 2 + zh_, zl_ * 2 + c_)

    home = zh == c

    q16[0:TOK, :] = q_ref[...]
    k16[0:TOK, :] = k_ref[...]
    v16[0:TOK, :] = v_ref[...]
    g16[0:TOK, :] = g_ref[...]
    hid[0:TOK, :] = res_ref[...]

    def out_peer(d):
        z2 = lax.rem(z + d, 8)
        zh2, zl2 = lax.div(z2, 4), lax.rem(z2, 4)
        return dev(x, y, zh2, zl2, zh), zl2 * 2 + zh2

    def in_peer(d):
        s = lax.rem(uly + d, 8)
        return dev(x, y, c, lax.div(s, 2), lax.rem(s, 2)), s

    other = dev(x, y, zh, zl, 1 - c)
    xto = lambda p: dev(p, y, zh, zl, c)
    yto = lambda p: dev(x, p, zh, zl, c)

    barrier = pltpu.get_barrier_semaphore()

    def greet(dest):
        pl.semaphore_signal(barrier, inc=1, device_id=dest, device_id_type=MESH)

    for d in range(1, NX):
        greet(xto(lax.rem(x + d, NX)))
    for d in (1, NY - 1):
        greet(yto(lax.rem(y + d, NY)))
    greet(other)
    for d in range(8):
        def both(d=d):
            greet(out_peer(d)[0])
            greet(in_peer(d)[0])
        if d == 0:
            pl.when(jnp.logical_not(home))(both)
        else:
            both()
    pl.when(home)(lambda: pl.semaphore_wait(barrier, 20))
    pl.when(jnp.logical_not(home))(lambda: pl.semaphore_wait(barrier, 22))

    if STAGE <= 1:
        out_ref[...] = res_ref[...]
        return
    order = (4, 3, 5, 2, 6, 1, 7, 0)

    def spread(src, dst, ss, rs):
        def make(d):
            dest, head = out_peer(d)
            return src(head), dst.at[uly], ss.at[d], rs.at[uly], dest
        return make

    def send_all(make):
        for d in order:
            s, t, a, b, dest = make(d)
            if d == 0:
                pl.when(home)(lambda s=s, t=t, b=b: pltpu.make_async_copy(s, t, b).start())
                pl.when(jnp.logical_not(home))(lambda s=s, t=t, a=a, b=b, dest=dest: remote(s, t, a, b, dest).start())
            else:
                remote(s, t, a, b, dest).start()

    def wait_all_sent(make):
        for d in order:
            s, t, a, b, dest = make(d)
            if d == 0:
                pl.when(jnp.logical_not(home))(lambda s=s, t=t, a=a, b=b, dest=dest: remote(s, t, a, b, dest).wait_send())
            else:
                remote(s, t, a, b, dest).wait_send()

    def wait_all_recv(dst, ss, rs):
        for i in range(8):
            remote(dst.at[i], dst.at[i], ss.at[i], rs.at[i], other).wait_recv()

    def cols(ref, width):
        return lambda head: ref.at[:, pl.ds(pl.multiple_of(head * width, 128), width)]

    moves = [
        spread(cols(k16, HEAD_SIZE), krec, a_ss.at[0], a_rs.at[0]),
        spread(cols(v16, HEAD_SIZE), vrec, a_ss.at[1], a_rs.at[1]),
        spread(cols(q16, GROUP * HEAD_SIZE), qrec, a_ss.at[2], a_rs.at[2]),
        spread(cols(g16, GROUP * HEAD_SIZE), grec, a_ss.at[3], a_rs.at[3]),
    ]
    send_all(moves[0])
    send_all(moves[1])

    weights = [(wo_ref, bufo), (wg_ref, bufg), (wu_ref, bufu), (wd_ref, bufd)]
    twin = dev(x, y, c, zl, zh)

    def swap(i):
        src, buf = weights[i]
        return src, buf.at[x, y, zh], w_ss.at[i], w_rs.at[i], twin

    def swap_start():
        for i in range(4):
            s, t, a, b, dest = swap(i)
            pl.when(home)(lambda s=s, t=t, b=b: pltpu.make_async_copy(s, t, b).start())
            pl.when(jnp.logical_not(home))(lambda s=s, t=t, a=a, b=b, dest=dest: remote(s, t, a, b, dest).start())

    def swap_wait(i):
        own = weights[i][1].at[x, y, c]
        remote(own, own, w_ss.at[i], w_rs.at[i], other).wait_recv()

    swap_start()
    send_all(moves[2])
    send_all(moves[3])

    def close(*makes):
        for m in moves + list(makes):
            wait_all_sent(m)
        for i in range(4):
            s, t, a, b, dest = swap(i)
            pl.when(jnp.logical_not(home))(lambda s=s, t=t, a=a, b=b, dest=dest: remote(s, t, a, b, dest).wait_send())
        for cp in sent:
            cp.wait_send()

    sent = []

    def gather(buf, idx, x_first, rows, theirs_too=True):
        rx = dict(n=NX, me=x, to=xto, ss=x_ss.at[idx], rs=x_rs.at[idx], log=sent)
        ry = dict(n=NY, me=y, to=yto, ss=y_ss.at[idx], rs=y_rs.at[idx], log=sent)
        hr = rows // 2
        if x_first:
            one = Direct(lambda i: buf.at[i, y, c], **rx)
            two = Ring(lambda i: buf.at[:, i, c], lambda i, w: buf.at[pl.ds(w * 2, 2), i, c], **ry)
        else:
            one = Ring(lambda i: buf.at[x, i, c], lambda i, w: buf.at[x, i, c, pl.ds(w * hr, hr)], **ry)
            two = Ring(lambda i: buf.at[i, :, c], lambda i, w: buf.at[i, pl.ds(w * 4, 4), c], **rx)

        def give(j, t):
            cp = remote(two.get(j), two.get(j), c_ss.at[idx, t], c_rs.at[idx, t], other)
            cp.start()
            sent.append(cp)

        one.start()
        yield
        if not x_first:
            for t in range(1, one.n // 2):
                one.step(t)
                yield
        one.finish()
        two.start()
        give(two.me, 0)
        yield
        for t in range(1, two.n // 2):
            two.step(t)
            give(two.pos(-t), 2 * t - 1)
            give(two.pos(t), 2 * t)
            yield
        two.finish()
        give(two.pos(two.n // 2), two.n - 1)
        yield
        if theirs_too:
            for t in range(two.n):
                theirs(buf, idx, x_first, t)
        yield

    def place(n, t):
        if t == n - 1:
            return n // 2
        return -((t + 1) // 2) if t % 2 else t // 2

    def theirs(buf, idx, x_first, t):
        if x_first:
            ref = buf.at[:, lax.rem(y + NY + place(NY, t), NY), 1 - c]
        else:
            ref = buf.at[lax.rem(x + NX + place(NX, t), NX), :, 1 - c]
        remote(ref, ref, c_ss.at[idx, t], c_rs.at[idx, t], other).wait_recv()

    def compact(rec, buf):
        for s in range(8):
            cmp_buf[TOK * s:TOK * (s + 1), :] = rec[s].astype(F32)[:TOK]
        buf[x, y, c] = cmp_buf[...].astype(BF16)

    gk = gather(bufk, 0, True, 96, False)
    gv = gather(bufv, 1, True, 96, False)
    go = gather(bufo, 2, False, 32)
    gg = gather(bufg, 3, False, 32)
    gu = gather(bufu, 4, True, 32)
    gd = gather(bufd, 5, False, 32)

    def go_on(*gens):
        for gen in gens:
            next(gen, None)

    scale = 1.0 / math.sqrt(HEAD_SIZE)

    def attend(first, last):
        for t in range(first, last):
            theirs(bufk, 0, True, t)
            theirs(bufv, 1, True, t)

        def body(i, _):
            far = lax.div(i + 1, 2)
            j = lax.rem(y + NY + jnp.where(jnp.logical_and(lax.rem(i, 2) == 1, i < NY - 1), -far, far), NY)
            keys = bufk[:, j].reshape(CHUNK, HEAD_SIZE)
            vals = bufv[:, j].reshape(CHUNK, HEAD_SIZE)
            visible = posk_ref[j] <= tq_ref[...]
            for g in range(GROUP):
                q = qrec[:, :, g * HEAD_SIZE:(g + 1) * HEAD_SIZE].reshape(8 * PAD, HEAD_SIZE)
                s = lax.dot_general(q, keys, (((1,), (1,)), ((), ())), preferred_element_type=F32) * scale
                s = jnp.where(visible, s, NEG)
                old = m_sc[g]
                new = jnp.maximum(old, jnp.max(s, axis=1, keepdims=True))
                p = jnp.exp(s - new)
                f = jnp.exp(old - new)
                l_sc[g] = l_sc[g] * f + jnp.sum(p, axis=1, keepdims=True)
                acc[g] = acc[g] * f + jnp.dot(p.astype(BF16), vals, preferred_element_type=F32)
                m_sc[g] = new
            return 0

        lax.fori_loop(first, last, body, 0)

    wait_all_recv(krec, a_ss.at[0], a_rs.at[0])
    compact(krec, bufk)
    go_on(gk)
    wait_all_recv(vrec, a_ss.at[1], a_rs.at[1])
    compact(vrec, bufv)
    go_on(gv)
    m_sc[...] = jnp.full_like(m_sc, NEG)
    l_sc[...] = jnp.zeros_like(l_sc)
    acc[...] = jnp.zeros_like(acc)
    swap_wait(0)
    go_on(go)
    go_on(gk, gv)
    go_on(go)
    for i in range(1, 4):
        swap_wait(i)
    go_on(gu)
    go_on(gk, gv)
    go_on(go)
    wait_all_recv(qrec, a_ss.at[2], a_rs.at[2])
    wait_all_recv(grec, a_ss.at[3], a_rs.at[3])
    attend(0, 1)
    go_on(gk, gv)
    go_on(go)
    go_on(gg)
    attend(1, 3)
    go_on(go)
    go_on(gk, gv)
    go_on(gd)
    go_on(gg)
    go_on(gu)
    attend(3, 5)
    go_on(gg, gd)
    go_on(go)
    go_on(gk, gv)
    attend(5, 7)
    go_on(gg, gd)
    go_on(go)
    attend(7, 8)
    for g in range(GROUP):
        gate = grec[:, :, g * HEAD_SIZE:(g + 1) * HEAD_SIZE].reshape(8 * PAD, HEAD_SIZE).astype(F32)
        gated[:, g * HEAD_SIZE:(g + 1) * HEAD_SIZE] = (acc[g] / l_sc[g] * jax.nn.sigmoid(gate)).astype(BF16)
    go_on(gg, gd)
    go_on(go)
    if STAGE <= 4:
        go_on(*[gg, gd, gu] * 9)
        out_ref[...] = res_ref[...]
        close()
        return

    NT = (((1,), (1,)), ((), ()))

    def collect(i, out, into, ss, rs):
        at = pl.ds(i * 384, 384)

        def make(d):
            dest, slot = in_peer(d)
            u = zl * 2 + zh
            return out.at[slot, :, at], into.at[u, :, at], ss.at[i, d], rs.at[i, u], dest
        return make

    def project(lhs, buf, width, out, into, ss, rs):
        makes = []
        for i in range(NX):
            part = lax.dot_general(lhs, buf[i].reshape(512, width), NT, preferred_element_type=F32)
            out[:, :, i * 384:(i + 1) * 384] = pack(part.reshape(8, PAD, 512)).astype(BF16)
            makes.append(collect(i, out, into, ss, rs))
            send_all(makes[-1])
        return makes

    def total(i, into, ss, rs):
        at = slice(i * 384, (i + 1) * 384)
        for u in range(8):
            ref = into.at[u, :, pl.ds(i * 384, 384)]
            remote(ref, ref, ss.at[i, u], rs.at[i, u], other).wait_recv()
        t = into[0, :, at].astype(F32)
        for u in range(1, 8):
            t = t + into[u, :, at].astype(F32)
        return unpack(t[None])[0]

    parts = project(gated[...], bufo, 512, pbuf, rbuf, r_ss, r_rs)
    go_on(gu)
    go_on(gd)
    square = jnp.zeros((PAD, 1), F32)
    for i in range(NX):
        at = slice(i * 512, (i + 1) * 512)
        h = (hid[:, at].astype(F32) + total(i, rbuf, r_ss, r_rs)).astype(BF16)
        hid[:, at] = h
        h = h.astype(F32)
        square += jnp.sum(h * h, axis=-1, keepdims=True)
    inv = lax.rsqrt(square * (1.0 / D) + 1e-06)
    for i in range(NX):
        at = slice(i * 512, (i + 1) * 512)
        nrm[:, i * 384:(i + 1) * 384] = pack((hid[:, at].astype(F32) * inv * gain_ref[:, at])[None])[0].astype(BF16)
    normed = spread(lambda head: nrm, nbuf, n_ss, n_rs)
    send_all(normed)
    go_on(gu)
    go_on(gg)
    go_on(gu)
    go_on(gd)
    go_on(gg)
    wait_all_recv(nbuf, n_ss, n_rs)
    for i in range(NX):
        at = slice(i * 512, (i + 1) * 512)
        rows[:, at] = unpack(nbuf[:, :, i * 384:(i + 1) * 384].astype(F32)).reshape(8 * PAD, 512).astype(BF16)
    if STAGE <= 7:
        go_on(*[gg, gd, gu] * 9)
        out_ref[...] = res_ref[...]
        close(normed, *parts)
        return
    go_on(gu)
    go_on(gg, gu)
    for n in range(FFC // 256):
        at = slice(n * 256, (n + 1) * 256)
        gate_sum = jnp.zeros((8 * PAD, 256), F32)
        up_sum = jnp.zeros((8 * PAD, 256), F32)
        for i in range(NX):
            r = rows[:, i * 512:(i + 1) * 512]
            gate_sum += jnp.dot(r, bufg[i, :, :, :, at].reshape(512, 256), preferred_element_type=F32)
            up_sum += jnp.dot(r, bufu[i, :, :, :, at].reshape(512, 256), preferred_element_type=F32)
        act[:, at] = (jax.nn.silu(gate_sum) * up_sum).astype(BF16)
    go_on(gd, gd)
    if STAGE <= 8:
        out_ref[...] = res_ref[...]
        close(normed, *parts)
        return
    parts += project(act[...], bufd, FFC, sbuf, fbuf, f_ss, f_rs)
    for i in range(NX):
        at = slice(i * 512, (i + 1) * 512)
        out_ref[:, at] = (hid[:, at].astype(F32) + total(i, fbuf, f_ss, f_rs))[:TOK].astype(BF16)
    close(normed, *parts)


def per_device(
    residual, query_projection, key_projection, value_projection, gate_proj, positions, prefix_len,
    out_weight, norm_gain, gate_weight, up_weight, down_weight,
):
    blk, uly = lax.axis_index("blk"), lax.axis_index("uly")
    first = (blk // 2 * 2 + uly % 2) * 96
    mine = lax.dynamic_slice_in_dim(positions, first, 96).reshape(8, TOK)
    tq = jnp.maximum(jnp.pad(mine, ((0, 0), (0, PAD - TOK))), prefix_len[0] - 1).reshape(8 * PAD, 1)
    posk = positions.reshape(NX, NY, CHUNK // NX).transpose(1, 0, 2).reshape(NY, 1, CHUNK)
    vm = pl.BlockSpec(memory_space=pltpu.VMEM)
    dma = pltpu.SemaphoreType.DMA
    half = lambda r, w: pltpu.VMEM((NX, NY, 2, r, w), BF16)
    return pl.pallas_call(
        kernel,
        out_shape=jax.ShapeDtypeStruct((TOK, D), BF16),
        in_specs=[vm] * 12,
        out_specs=vm,
        scratch_shapes=[
            pltpu.VMEM((PAD, 4096), BF16),
            pltpu.VMEM((PAD, 1024), BF16),
            pltpu.VMEM((PAD, 1024), BF16),
            pltpu.VMEM((PAD, 4096), BF16),
            pltpu.VMEM((8, PAD, 128), BF16),
            pltpu.VMEM((8, PAD, 128), BF16),
            pltpu.VMEM((8, PAD, 512), BF16),
            pltpu.VMEM((8, PAD, 512), BF16),
            pltpu.VMEM((96, 128), F32),
            half(96, 128), half(96, 128), half(32, 512), half(32, FFC), half(32, FFC), half(32, FFC),
            pltpu.VMEM((GROUP, 8 * PAD, 1), F32),
            pltpu.VMEM((GROUP, 8 * PAD, 1), F32),
            pltpu.VMEM((GROUP, 8 * PAD, HEAD_SIZE), F32),
            pltpu.VMEM((8 * PAD, GROUP * HEAD_SIZE), BF16),
            pltpu.VMEM((8, PAD, 1536), BF16),
            pltpu.VMEM((8, PAD, 1536), BF16),
            pltpu.VMEM((8, PAD, 1536), BF16),
            pltpu.VMEM((8, PAD, 1536), BF16),
            pltpu.VMEM((PAD, D), BF16),
            pltpu.VMEM((PAD, 1536), BF16),
            pltpu.VMEM((8, PAD, 1536), BF16),
            pltpu.VMEM((8 * PAD, D), BF16),
            pltpu.VMEM((8 * PAD, FFC), BF16),
            dma((4, 8)), dma((4, 8)),
            dma((4,)), dma((4,)),
            dma((6, 2, 2)), dma((6, 2, 2)),
            dma((6, 2, 4)), dma((6, 2, 4)),
            dma((6, 8)), dma((6, 8)),
            dma((4, 8)), dma((4, 8)),
            dma((8,)), dma((8,)),
            dma((4, 8)), dma((4, 8)),
        ],
        compiler_params=pltpu.CompilerParams(
            collective_id=0, has_side_effects=True, vmem_limit_bytes=60 * 2**20
        ),
        name="layer",
    )(
        query_projection, key_projection, value_projection, gate_proj, residual, tq, posk,
        norm_gain.reshape(1, D), out_weight.T, gate_weight, up_weight, down_weight.T,
    )


def solution(mesh):
    return jax.shard_map(
        per_device,
        mesh=mesh,
        in_specs=(
            P(("blk", "uly"), None),
            P(("blk", "uly"), None),
            P(("blk", "uly"), None),
            P(("blk", "uly"), None),
            P(("blk", "uly"), None),
            P(),
            P(),
            P("uly", "blk"),
            P(),
            P("blk", "uly"),
            P("blk", "uly"),
            P("uly", "blk"),
        ),
        out_specs=P(("blk", "uly"), None),
        check_vma=False,
    )
```

```python
import functools
import math

import jax
import jax.numpy as jnp
from jax import lax
from jax.experimental import pallas as pl
from jax.experimental.pallas import tpu as pltpu
from jax.sharding import PartitionSpec as P

MESH = pl.DeviceIdType.MESH
HEAD_SIZE = 128
GROUP = 4
NX, NY = 4, 8
TOK = 12
PAD = 16
D = 2048
FFC = 768
CHUNK = 768
F32 = jnp.float32
BF16 = jnp.bfloat16
NEG = -1e30
STAGE = 99


def remote(src, dst, ss, rs, dest):
    return pltpu.make_async_remote_copy(
        src_ref=src, dst_ref=dst, send_sem=ss, recv_sem=rs, device_id=dest, device_id_type=MESH
    )


class Ring:
    def __init__(self, get, half, me, n, to, ss, rs, log):
        self.get, self.half, self.me, self.n, self.to, self.ss, self.rs = get, half, me, n, to, ss, rs
        self.sent = log

    def pos(self, d):
        return lax.rem(self.me + (d + self.n), self.n)

    def send(self, ref, way, t):
        step = 1 if way == 0 else -1
        cp = remote(ref, ref, self.ss.at[way, t], self.rs.at[way, t], self.to(self.pos(step)))
        cp.start()
        self.sent.append(cp)

    def wait(self, ref, way, t):
        remote(ref, ref, self.ss.at[way, t], self.rs.at[way, t], self.to(self.pos(1))).wait_recv()

    def start(self):
        own = self.get(self.me)
        self.send(own, 0, 0)
        self.send(own, 1, 0)

    def step(self, t):
        h = self.n // 2
        for way in (0, 1):
            j = self.pos(-t if way == 0 else t)
            self.wait(self.get(j), way, t - 1)
            self.send(self.get(j) if t < h - 1 else self.half(j, way), way, t)

    def finish(self):
        h = self.n // 2
        j = self.pos(h)
        for way in (0, 1):
            self.wait(self.half(j, way), way, h - 1)


class Direct:
    def __init__(self, get, me, n, to, ss, rs, log):
        self.get, self.me, self.n, self.to, self.ss, self.rs, self.sent = get, me, n, to, ss, rs, log

    def pos(self, d):
        return lax.rem(self.me + d, self.n)

    def start(self):
        own = self.get(self.me)
        for d in range(1, self.n):
            cp = remote(own, own, self.ss.at[d // 2, d % 2], self.rs.at[d // 2, d % 2], self.to(self.pos(d)))
            cp.start()
            self.sent.append(cp)

    def finish(self):
        for d in range(1, self.n):
            ref = self.get(self.pos(self.n - d))
            remote(ref, ref, self.ss.at[d // 2, d % 2], self.rs.at[d // 2, d % 2], self.to(self.pos(1))).wait_recv()


def pack(v):
    lo, hi = v[:, :8], v[:, 8:]
    turn = lambda t: jnp.concatenate([t[:, 4:], t[:, :4]], axis=1)
    extra = jnp.concatenate([turn(lo[..., 384:]), lo[..., 384:], turn(hi[..., 384:])], axis=2)
    row = lax.broadcasted_iota(jnp.int32, extra.shape, 1)
    return jnp.concatenate([lo[..., :384], jnp.where(row < 4, hi[..., :384], extra)], axis=1)


def unpack(v):
    lo, hi = v[:, :8], v[:, 8:]
    turn = lambda t: jnp.concatenate([t[:, 4:], t[:, :4]], axis=1)
    a, b, d = hi[..., :128], hi[..., 128:256], hi[..., 256:]
    row = lax.broadcasted_iota(jnp.int32, a.shape, 1)
    last = jnp.concatenate([jnp.where(row < 4, turn(a), b), turn(d)], axis=1)
    return jnp.concatenate([v, last], axis=2)


def kernel(
    q_ref, k_ref, v_ref, g_ref, res_ref, tq_ref, posa_ref, posb_ref, gain_ref, wo_ref, wg_ref, wu_ref, wd_ref,
    out_ref,
    q16, k16, v16, g16, krec, vrec, qrec, grec, cmp_buf,
    bufk, bufo, bufg, bufu, bufd,
    m_sc, l_sc, acc, gated, pbuf, rbuf, sbuf, fbuf, hid, nrm, nbuf, rows, act,
    a_ss, a_rs, w_ss, w_rs, x_ss, x_rs, y_ss, y_rs, c_ss, c_rs, r_ss, r_rs, n_ss, n_rs, f_ss, f_rs,
):
    blk, uly = lax.axis_index("blk"), lax.axis_index("uly")
    x, y, zh = lax.div(blk, 16), lax.rem(lax.div(blk, 2), 8), lax.rem(blk, 2)
    zl, c = lax.div(uly, 2), lax.rem(uly, 2)
    z = zh * 4 + zl

    def dev(x_, y_, zh_, zl_, c_):
        return ((x_ * NY + y_) * 2 + zh_, zl_ * 2 + c_)

    home = zh == c


    def out_peer(d):
        z2 = lax.rem(z + d, 8)
        zh2, zl2 = lax.div(z2, 4), lax.rem(z2, 4)
        return dev(x, y, zh2, zl2, zh), zl2 * 2 + zh2

    def in_peer(d):
        s = lax.rem(uly + d, 8)
        return dev(x, y, c, lax.div(s, 2), lax.rem(s, 2)), s

    other = dev(x, y, zh, zl, 1 - c)
    xto = lambda p: dev(p, y, zh, zl, c)
    yto = lambda p: dev(x, p, zh, zl, c)

    barrier = pltpu.get_barrier_semaphore()

    def greet(dest):
        pl.semaphore_signal(barrier, inc=1, device_id=dest, device_id_type=MESH)

    for d in range(1, NX):
        greet(xto(lax.rem(x + d, NX)))
    for d in (1, NY - 1):
        greet(yto(lax.rem(y + d, NY)))
    greet(other)
    for d in range(8):
        def both(d=d):
            greet(out_peer(d)[0])
            greet(in_peer(d)[0])
        if d == 0:
            pl.when(jnp.logical_not(home))(both)
        else:
            both()
    q16[0:TOK, :] = q_ref[...]
    k16[0:TOK, :] = k_ref[...]
    v16[0:TOK, :] = v_ref[...]
    g16[0:TOK, :] = g_ref[...]
    hid[0:TOK, :] = res_ref[...]
    pl.when(home)(lambda: pl.semaphore_wait(barrier, 20))
    pl.when(jnp.logical_not(home))(lambda: pl.semaphore_wait(barrier, 22))

    if STAGE <= 1:
        out_ref[...] = res_ref[...]
        return
    order = (4, 3, 5, 2, 6, 1, 7, 0)

    def spread(src, dst, ss, rs):
        def make(d):
            dest, head = out_peer(d)
            return src(head), dst.at[uly], ss.at[d], rs.at[uly], dest
        return make

    def send_all(make):
        for d in order:
            s, t, a, b, dest = make(d)
            if d == 0:
                pl.when(home)(lambda s=s, t=t, b=b: pltpu.make_async_copy(s, t, b).start())
                pl.when(jnp.logical_not(home))(lambda s=s, t=t, a=a, b=b, dest=dest: remote(s, t, a, b, dest).start())
            else:
                remote(s, t, a, b, dest).start()

    def wait_all_sent(make):
        for d in order:
            s, t, a, b, dest = make(d)
            if d == 0:
                pl.when(jnp.logical_not(home))(lambda s=s, t=t, a=a, b=b, dest=dest: remote(s, t, a, b, dest).wait_send())
            else:
                remote(s, t, a, b, dest).wait_send()

    def wait_all_recv(dst, ss, rs):
        for i in range(8):
            remote(dst.at[i], dst.at[i], ss.at[i], rs.at[i], other).wait_recv()

    def cols(ref, width):
        return lambda head: ref.at[:, pl.ds(pl.multiple_of(head * width, 128), width)]

    moves = [
        spread(cols(k16, HEAD_SIZE), krec, a_ss.at[0], a_rs.at[0]),
        spread(cols(v16, HEAD_SIZE), vrec, a_ss.at[1], a_rs.at[1]),
        spread(cols(q16, GROUP * HEAD_SIZE), qrec, a_ss.at[2], a_rs.at[2]),
        spread(cols(g16, GROUP * HEAD_SIZE), grec, a_ss.at[3], a_rs.at[3]),
    ]
    weights = [(wo_ref, bufo), (wg_ref, bufg), (wu_ref, bufu), (wd_ref, bufd)]
    twin = dev(x, y, c, zl, zh)

    def swap(i):
        src, buf = weights[i]
        return src, buf.at[x, y, zh], w_ss.at[i], w_rs.at[i], twin

    def swap_start(first, last):
        for i in range(first, last):
            s, t, a, b, dest = swap(i)
            pl.when(home)(lambda s=s, t=t, b=b: pltpu.make_async_copy(s, t, b).start())
            pl.when(jnp.logical_not(home))(lambda s=s, t=t, a=a, b=b, dest=dest: remote(s, t, a, b, dest).start())

    def swap_wait(i):
        own = weights[i][1].at[x, y, c]
        remote(own, own, w_ss.at[i], w_rs.at[i], other).wait_recv()

    swap_start(0, 1)
    send_all(moves[0])
    send_all(moves[1])
    swap_start(1, 4)
    send_all(moves[2])
    send_all(moves[3])

    def close(*makes):
        for m in moves + list(makes):
            wait_all_sent(m)
        for i in range(4):
            s, t, a, b, dest = swap(i)
            pl.when(jnp.logical_not(home))(lambda s=s, t=t, a=a, b=b, dest=dest: remote(s, t, a, b, dest).wait_send())
        for cp in sent:
            cp.wait_send()

    sent = []

    def gather(buf, idx, x_first, at=(), halves=None, theirs_too=True):
        rx = dict(n=NX, me=x, to=xto, ss=x_ss.at[idx], rs=x_rs.at[idx], log=sent)
        ry = dict(n=NY, me=y, to=yto, ss=y_ss.at[idx], rs=y_rs.at[idx], log=sent)
        if x_first:
            one = Direct(lambda i: buf.at[(i, y, c) + at], **rx)
            two = Ring(lambda i: buf.at[(slice(None), i, c) + at], lambda i, w: buf.at[(pl.ds(w * 2, 2), i, c) + at], **ry)
        else:
            one = Ring(lambda i: buf.at[(x, i, c) + at], lambda i, w: buf.at[(x, i, c) + halves(w)], **ry)
            two = Ring(lambda i: buf.at[(i, slice(None), c) + at], lambda i, w: buf.at[(i, pl.ds(w * 4, 4), c) + at], **rx)

        def give(j, t):
            cp = remote(two.get(j), two.get(j), c_ss.at[idx, t], c_rs.at[idx, t], other)
            cp.start()
            sent.append(cp)

        one.start()
        yield
        if not x_first:
            for t in range(1, one.n // 2):
                one.step(t)
                yield
        one.finish()
        two.start()
        give(two.me, 0)
        yield
        for t in range(1, two.n // 2):
            two.step(t)
            give(two.pos(-t), 2 * t - 1)
            give(two.pos(t), 2 * t)
            yield
        two.finish()
        give(two.pos(two.n // 2), two.n - 1)
        yield
        if theirs_too:
            for t in range(two.n):
                theirs(buf, idx, x_first, t, at)
        yield

    def place(n, t):
        if t == n - 1:
            return n // 2
        return -((t + 1) // 2) if t % 2 else t // 2

    def spot(x_first, t):
        if x_first:
            return lax.rem(y + NY + place(NY, t), NY)
        return lax.rem(x + NX + place(NX, t), NX)

    def theirs(buf, idx, x_first, t, at):
        j = spot(x_first, t)
        ref = buf.at[((slice(None), j) if x_first else (j, slice(None))) + (1 - c,) + at]
        remote(ref, ref, c_ss.at[idx, t], c_rs.at[idx, t], other).wait_recv()

    def compact(rec, i):
        for s in range(8):
            cmp_buf[TOK * s:TOK * (s + 1), :] = rec[s].astype(F32)[:TOK]
        bufk[x, y, c, i] = cmp_buf[...].astype(BF16)

    every = slice(None)
    k_at = [(every, pl.ds(0, 48)), (every, pl.ds(48, 48))]
    ka = gather(bufk, 0, True, k_at[0], theirs_too=False)
    kb = gather(bufk, 1, False, k_at[1], lambda w: (pl.ds(w, 1), pl.ds(48, 48)), theirs_too=False)
    oa = gather(bufo, 2, True, (pl.ds(0, 16),))
    ob = gather(bufo, 3, False, (pl.ds(16, 16),), lambda w: (pl.ds(16, 16), pl.ds(w * 256, 256)))
    gg = gather(bufg, 4, False, (), lambda w: (pl.ds(w * 16, 16),))
    gu = gather(bufu, 5, True)
    gd = gather(bufd, 6, False, (), lambda w: (pl.ds(w * 16, 16),))

    def go_on(*gens):
        for gen in gens:
            next(gen, None)

    power = math.log2(math.e) / math.sqrt(HEAD_SIZE)
    ones = jnp.ones((CHUNK, HEAD_SIZE), BF16)

    def attend(x_first, *arrivals):
        keys, vals, pos = [], [], []
        for t in arrivals:
            theirs(bufk, 0 if x_first else 1, x_first, t, k_at[0 if x_first else 1])
        for t in arrivals:
            j = spot(x_first, t)
            if x_first:
                keys.append(bufk[:, j, :, 0, 0:48].reshape(CHUNK // 2, HEAD_SIZE))
                vals.append(bufk[:, j, :, 1, 0:48].reshape(CHUNK // 2, HEAD_SIZE))
                pos.append(posa_ref[j])
            else:
                keys.append(bufk[j, :, :, 0, 48:96].reshape(CHUNK, HEAD_SIZE))
                vals.append(bufk[j, :, :, 1, 48:96].reshape(CHUNK, HEAD_SIZE))
                pos.append(posb_ref[j])
        join = lambda parts, axis: parts[0] if len(parts) == 1 else jnp.concatenate(parts, axis)
        keys, vals = join(keys, 0), jnp.concatenate([join(vals, 0), ones], 1)
        visible = join(pos, 1) <= tq_ref[...]
        for g in range(GROUP):
            q = qrec[:, :, g * HEAD_SIZE:(g + 1) * HEAD_SIZE].reshape(8 * PAD, HEAD_SIZE)
            s = lax.dot_general(q, keys, (((1,), (1,)), ((), ())), preferred_element_type=F32)
            s = jnp.where(visible, s, NEG)
            old = m_sc[g]
            new = jnp.maximum(old, jnp.broadcast_to(jnp.max(s, axis=1, keepdims=True), old.shape))
            p = jnp.exp2((s - jnp.concatenate([new] * (CHUNK // HEAD_SIZE), 1)) * power)
            f = jnp.exp2((old - new) * power)
            o = jnp.dot(p.astype(BF16), vals, preferred_element_type=F32)
            l_sc[g] = l_sc[g] * f + o[:, HEAD_SIZE:]
            acc[g] = acc[g] * f + o[:, :HEAD_SIZE]
            m_sc[g] = new

    swap_wait(0)
    go_on(oa, ob)
    wait_all_recv(krec, a_ss.at[0], a_rs.at[0])
    compact(krec, 0)
    wait_all_recv(vrec, a_ss.at[1], a_rs.at[1])
    compact(vrec, 1)
    go_on(kb, ka)
    m_sc[...] = jnp.full_like(m_sc, NEG)
    l_sc[...] = jnp.zeros_like(l_sc)
    acc[...] = jnp.zeros_like(acc)
    go_on(ob, kb, ka, oa)
    go_on(ob, kb)
    for i in range(1, 4):
        swap_wait(i)
    go_on(ka, ob, kb)
    go_on(oa, ka)
    go_on(kb, ob)
    go_on(gg, gu)
    wait_all_recv(qrec, a_ss.at[2], a_rs.at[2])
    wait_all_recv(grec, a_ss.at[3], a_rs.at[3])
    attend(True, 1, 2)
    go_on(ka, oa)
    go_on(gg, gd)
    attend(False, 0)
    go_on(kb)
    attend(True, 3, 4)
    go_on(ob)
    go_on(gg, gd)
    go_on(ka, oa)
    attend(True, 5, 6)
    go_on(gg, gd)
    go_on(gu)
    attend(False, 1)
    go_on(kb)
    attend(False, 2)
    go_on(gg)
    go_on(oa, ob)
    attend(True, 0, 7)
    go_on(gd)
    attend(False, 3)
    go_on(gu, gd)
    go_on(oa, ob)
    for g in range(GROUP):
        gate = grec[:, :, g * HEAD_SIZE:(g + 1) * HEAD_SIZE].reshape(8 * PAD, HEAD_SIZE).astype(F32)
        gated[:, g * HEAD_SIZE:(g + 1) * HEAD_SIZE] = (acc[g] / l_sc[g] * jax.nn.sigmoid(gate)).astype(BF16)
    if STAGE <= 4:
        go_on(*[gg, gd, gu] * 9)
        out_ref[...] = res_ref[...]
        close()
        return

    NT = (((1,), (1,)), ((), ()))

    def collect(i, out, into, ss, rs):
        at = pl.ds(i * 384, 384)

        def make(d):
            dest, slot = in_peer(d)
            u = zl * 2 + zh
            return out.at[slot, :, at], into.at[u, :, at], ss.at[i, d], rs.at[i, u], dest
        return make

    def project(lhs, buf, width, out, into, ss, rs):
        makes = []
        for i in range(NX):
            part = lax.dot_general(lhs, buf[i].reshape(512, width), NT, preferred_element_type=F32)
            out[:, :, i * 384:(i + 1) * 384] = pack(part.reshape(8, PAD, 512)).astype(BF16)
            makes.append(collect(i, out, into, ss, rs))
            send_all(makes[-1])
        return makes

    def total(i, into, ss, rs):
        at = slice(i * 384, (i + 1) * 384)
        for u in range(8):
            ref = into.at[u, :, pl.ds(i * 384, 384)]
            remote(ref, ref, ss.at[i, u], rs.at[i, u], other).wait_recv()
        t = into[0, :, at].astype(F32)
        for u in range(1, 8):
            t = t + into[u, :, at].astype(F32)
        return unpack(t[None])[0]

    parts = project(gated[...], bufo, 512, pbuf, rbuf, r_ss, r_rs)
    go_on(gu)
    go_on(gg)
    square = jnp.zeros((PAD, 1), F32)
    for i in range(NX):
        at = slice(i * 512, (i + 1) * 512)
        h = (hid[:, at].astype(F32) + total(i, rbuf, r_ss, r_rs)).astype(BF16)
        hid[:, at] = h
        h = h.astype(F32)
        square += jnp.sum(h * h, axis=-1, keepdims=True)
    inv = lax.rsqrt(square * (1.0 / D) + 1e-06)
    for i in range(NX):
        at = slice(i * 512, (i + 1) * 512)
        nrm[:, i * 384:(i + 1) * 384] = pack((hid[:, at].astype(F32) * inv * gain_ref[:, at])[None])[0].astype(BF16)
    normed = spread(lambda head: nrm, nbuf, n_ss, n_rs)
    send_all(normed)
    go_on(gu)
    go_on(gg)
    go_on(gu)
    go_on(gd)
    wait_all_recv(nbuf, n_ss, n_rs)
    for i in range(NX):
        at = slice(i * 512, (i + 1) * 512)
        rows[:, at] = unpack(nbuf[:, :, i * 384:(i + 1) * 384].astype(F32)).reshape(8 * PAD, 512).astype(BF16)
    if STAGE <= 7:
        go_on(*[gg, gd, gu] * 9)
        out_ref[...] = res_ref[...]
        close(normed, *parts)
        return
    go_on(gg, gu)
    for n in range(FFC // 256):
        at = slice(n * 256, (n + 1) * 256)
        gate_sum = jnp.zeros((8 * PAD, 256), F32)
        up_sum = jnp.zeros((8 * PAD, 256), F32)
        for i in range(NX):
            r = rows[:, i * 512:(i + 1) * 512]
            gate_sum += jnp.dot(r, bufg[i, :, :, :, at].reshape(512, 256), preferred_element_type=F32)
            up_sum += jnp.dot(r, bufu[i, :, :, :, at].reshape(512, 256), preferred_element_type=F32)
        act[:, at] = (jax.nn.silu(gate_sum) * up_sum).astype(BF16)
    go_on(gd, gd)
    if STAGE <= 8:
        out_ref[...] = res_ref[...]
        close(normed, *parts)
        return
    parts += project(act[...], bufd, FFC, sbuf, fbuf, f_ss, f_rs)
    for i in range(NX):
        at = slice(i * 512, (i + 1) * 512)
        out_ref[:, at] = (hid[:, at].astype(F32) + total(i, fbuf, f_ss, f_rs))[:TOK].astype(BF16)
    close(normed, *parts)


def per_device(
    residual, query_projection, key_projection, value_projection, gate_proj, positions, prefix_len,
    out_weight, norm_gain, gate_weight, up_weight, down_weight,
):
    blk, uly = lax.axis_index("blk"), lax.axis_index("uly")
    first = (blk // 2 * 2 + uly % 2) * 96
    mine = lax.dynamic_slice_in_dim(positions, first, 96).reshape(8, TOK)
    tq = jnp.maximum(jnp.pad(mine, ((0, 0), (0, PAD - TOK))), prefix_len[0] - 1).reshape(8 * PAD, 1)
    pos = positions.reshape(NX, NY, 2, 2, 48)
    posa = pos[:, :, :, 0].transpose(1, 0, 2, 3).reshape(NY, 1, CHUNK // 2)
    posb = pos[:, :, :, 1].reshape(NX, 1, CHUNK)
    vm = pl.BlockSpec(memory_space=pltpu.VMEM)
    dma = pltpu.SemaphoreType.DMA
    half = lambda r, w: pltpu.VMEM((NX, NY, 2, r, w), BF16)
    return pl.pallas_call(
        kernel,
        out_shape=jax.ShapeDtypeStruct((TOK, D), BF16),
        in_specs=[vm] * 13,
        out_specs=vm,
        scratch_shapes=[
            pltpu.VMEM((PAD, 4096), BF16),
            pltpu.VMEM((PAD, 1024), BF16),
            pltpu.VMEM((PAD, 1024), BF16),
            pltpu.VMEM((PAD, 4096), BF16),
            pltpu.VMEM((8, PAD, 128), BF16),
            pltpu.VMEM((8, PAD, 128), BF16),
            pltpu.VMEM((8, PAD, 512), BF16),
            pltpu.VMEM((8, PAD, 512), BF16),
            pltpu.VMEM((96, 128), F32),
            pltpu.VMEM((NX, NY, 2, 2, 96, 128), BF16), half(32, 512), half(32, FFC), half(32, FFC), half(32, FFC),
            pltpu.VMEM((GROUP, 8 * PAD, HEAD_SIZE), F32),
            pltpu.VMEM((GROUP, 8 * PAD, HEAD_SIZE), F32),
            pltpu.VMEM((GROUP, 8 * PAD, HEAD_SIZE), F32),
            pltpu.VMEM((8 * PAD, GROUP * HEAD_SIZE), BF16),
            pltpu.VMEM((8, PAD, 1536), BF16),
            pltpu.VMEM((8, PAD, 1536), BF16),
            pltpu.VMEM((8, PAD, 1536), BF16),
            pltpu.VMEM((8, PAD, 1536), BF16),
            pltpu.VMEM((PAD, D), BF16),
            pltpu.VMEM((PAD, 1536), BF16),
            pltpu.VMEM((8, PAD, 1536), BF16),
            pltpu.VMEM((8 * PAD, D), BF16),
            pltpu.VMEM((8 * PAD, FFC), BF16),
            dma((4, 8)), dma((4, 8)),
            dma((4,)), dma((4,)),
            dma((7, 2, 2)), dma((7, 2, 2)),
            dma((7, 2, 4)), dma((7, 2, 4)),
            dma((7, 8)), dma((7, 8)),
            dma((4, 8)), dma((4, 8)),
            dma((8,)), dma((8,)),
            dma((4, 8)), dma((4, 8)),
        ],
        compiler_params=pltpu.CompilerParams(
            collective_id=0, has_side_effects=True, vmem_limit_bytes=60 * 2**20
        ),
        name="layer",
    )(
        query_projection, key_projection, value_projection, gate_proj, residual, tq, posa, posb,
        norm_gain.reshape(1, D), out_weight.T, gate_weight, up_weight, down_weight.T,
    )


def solution(mesh):
    return jax.shard_map(
        per_device,
        mesh=mesh,
        in_specs=(
            P(("blk", "uly"), None),
            P(("blk", "uly"), None),
            P(("blk", "uly"), None),
            P(("blk", "uly"), None),
            P(("blk", "uly"), None),
            P(),
            P(),
            P("uly", "blk"),
            P(),
            P("blk", "uly"),
            P("blk", "uly"),
            P("uly", "blk"),
        ),
        out_specs=P(("blk", "uly"), None),
        check_vma=False,
    )
```

```python
import functools
import math

import jax
import jax.numpy as jnp
from jax import lax
from jax.experimental import pallas as pl
from jax.experimental.pallas import tpu as pltpu
from jax.sharding import PartitionSpec as P

MESH = pl.DeviceIdType.MESH
HEAD_SIZE = 128
GROUP = 4
NX, NY = 4, 8
TOK = 12
PAD = 16
D = 2048
FFC = 768
CHUNK = 768
F32 = jnp.float32
BF16 = jnp.bfloat16
NEG = -1e30


def remote(src, dst, ss, rs, dest):
    return pltpu.make_async_remote_copy(
        src_ref=src, dst_ref=dst, send_sem=ss, recv_sem=rs, device_id=dest, device_id_type=MESH
    )


class Ring:
    def __init__(self, get, half, me, n, to, ss, rs, log):
        self.get, self.half, self.me, self.n, self.to, self.ss, self.rs = get, half, me, n, to, ss, rs
        self.sent = log

    def pos(self, d):
        return lax.rem(self.me + (d + self.n), self.n)

    def send(self, ref, way, t):
        step = 1 if way == 0 else -1
        cp = remote(ref, ref, self.ss.at[way, t], self.rs.at[way, t], self.to(self.pos(step)))
        cp.start()
        self.sent.append(cp)

    def wait(self, ref, way, t):
        remote(ref, ref, self.ss.at[way, t], self.rs.at[way, t], self.to(self.pos(1))).wait_recv()

    def start(self):
        own = self.get(self.me)
        self.send(own, 0, 0)
        self.send(own, 1, 0)

    def step(self, t):
        h = self.n // 2
        for way in (0, 1):
            j = self.pos(-t if way == 0 else t)
            self.wait(self.get(j), way, t - 1)
            self.send(self.get(j) if t < h - 1 else self.half(j, way), way, t)

    def finish(self):
        h = self.n // 2
        j = self.pos(h)
        for way in (0, 1):
            self.wait(self.half(j, way), way, h - 1)


class Direct:
    def __init__(self, get, me, n, to, ss, rs, log):
        self.get, self.me, self.n, self.to, self.ss, self.rs, self.sent = get, me, n, to, ss, rs, log

    def pos(self, d):
        return lax.rem(self.me + d, self.n)

    def start(self):
        own = self.get(self.me)
        for d in range(1, self.n):
            cp = remote(own, own, self.ss.at[d // 2, d % 2], self.rs.at[d // 2, d % 2], self.to(self.pos(d)))
            cp.start()
            self.sent.append(cp)

    def finish(self):
        for d in range(1, self.n):
            ref = self.get(self.pos(self.n - d))
            remote(ref, ref, self.ss.at[d // 2, d % 2], self.rs.at[d // 2, d % 2], self.to(self.pos(1))).wait_recv()


def pack(v):
    lo, hi = v[:, :8], v[:, 8:]
    turn = lambda t: jnp.concatenate([t[:, 4:], t[:, :4]], axis=1)
    extra = jnp.concatenate([turn(lo[..., 384:]), lo[..., 384:], turn(hi[..., 384:])], axis=2)
    row = lax.broadcasted_iota(jnp.int32, extra.shape, 1)
    return jnp.concatenate([lo[..., :384], jnp.where(row < 4, hi[..., :384], extra)], axis=1)


def unpack(v):
    lo, hi = v[:, :8], v[:, 8:]
    turn = lambda t: jnp.concatenate([t[:, 4:], t[:, :4]], axis=1)
    a, b, d = hi[..., :128], hi[..., 128:256], hi[..., 256:]
    row = lax.broadcasted_iota(jnp.int32, a.shape, 1)
    last = jnp.concatenate([jnp.where(row < 4, turn(a), b), turn(d)], axis=1)
    return jnp.concatenate([v, last], axis=2)


def kernel(
    q_ref, k_ref, v_ref, g_ref, res_ref, tq_ref, posa_ref, posb_ref, gain_ref, wo_ref, wg_ref, wu_ref, wd_ref,
    out_ref,
    q16, k16, v16, g16, krec, vrec, qrec, grec, cmp_buf,
    bufk, bufo, bufg, bufu, bufd,
    m_sc, l_sc, acc, gated, pbuf, rbuf, sbuf, fbuf, hid, nrm, nbuf, rows, act,
    a_ss, a_rs, w_ss, w_rs, x_ss, x_rs, y_ss, y_rs, c_ss, c_rs, r_ss, r_rs, n_ss, n_rs, f_ss, f_rs,
):
    blk, uly = lax.axis_index("blk"), lax.axis_index("uly")
    x, y, zh = lax.div(blk, 16), lax.rem(lax.div(blk, 2), 8), lax.rem(blk, 2)
    zl, c = lax.div(uly, 2), lax.rem(uly, 2)
    z = zh * 4 + zl

    def dev(x_, y_, zh_, zl_, c_):
        return ((x_ * NY + y_) * 2 + zh_, zl_ * 2 + c_)

    home = zh == c


    def out_peer(d):
        z2 = lax.rem(z + d, 8)
        zh2, zl2 = lax.div(z2, 4), lax.rem(z2, 4)
        return dev(x, y, zh2, zl2, zh), zl2 * 2 + zh2

    def in_peer(d):
        s = lax.rem(uly + d, 8)
        return dev(x, y, c, lax.div(s, 2), lax.rem(s, 2)), s

    other = dev(x, y, zh, zl, 1 - c)
    xto = lambda p: dev(p, y, zh, zl, c)
    yto = lambda p: dev(x, p, zh, zl, c)

    barrier = pltpu.get_barrier_semaphore()

    def greet(dest):
        pl.semaphore_signal(barrier, inc=1, device_id=dest, device_id_type=MESH)

    for d in range(1, NX):
        greet(xto(lax.rem(x + d, NX)))
    for d in (1, NY - 1):
        greet(yto(lax.rem(y + d, NY)))
    greet(other)
    for d in range(8):
        def both(d=d):
            greet(out_peer(d)[0])
            greet(in_peer(d)[0])
        if d == 0:
            pl.when(jnp.logical_not(home))(both)
        else:
            both()
    q16[0:TOK, :] = q_ref[...]
    k16[0:TOK, :] = k_ref[...]
    v16[0:TOK, :] = v_ref[...]
    g16[0:TOK, :] = g_ref[...]
    hid[0:TOK, :] = res_ref[...]
    pl.when(home)(lambda: pl.semaphore_wait(barrier, 20))
    pl.when(jnp.logical_not(home))(lambda: pl.semaphore_wait(barrier, 22))

    order = (4, 3, 5, 2, 6, 1, 7, 0)

    def spread(src, dst, ss, rs):
        def make(d):
            dest, head = out_peer(d)
            return src(head), dst.at[uly], ss.at[d], rs.at[uly], dest
        return make

    def send_all(make):
        for d in order:
            s, t, a, b, dest = make(d)
            if d == 0:
                pl.when(home)(lambda s=s, t=t, b=b: pltpu.make_async_copy(s, t, b).start())
                pl.when(jnp.logical_not(home))(lambda s=s, t=t, a=a, b=b, dest=dest: remote(s, t, a, b, dest).start())
            else:
                remote(s, t, a, b, dest).start()

    def wait_all_sent(make):
        for d in order:
            s, t, a, b, dest = make(d)
            if d == 0:
                pl.when(jnp.logical_not(home))(lambda s=s, t=t, a=a, b=b, dest=dest: remote(s, t, a, b, dest).wait_send())
            else:
                remote(s, t, a, b, dest).wait_send()

    def wait_all_recv(dst, ss, rs):
        for i in range(8):
            remote(dst.at[i], dst.at[i], ss.at[i], rs.at[i], other).wait_recv()

    def cols(ref, width):
        return lambda head: ref.at[:, pl.ds(pl.multiple_of(head * width, 128), width)]

    moves = [
        spread(cols(k16, HEAD_SIZE), krec, a_ss.at[0], a_rs.at[0]),
        spread(cols(v16, HEAD_SIZE), vrec, a_ss.at[1], a_rs.at[1]),
        spread(cols(q16, GROUP * HEAD_SIZE), qrec, a_ss.at[2], a_rs.at[2]),
        spread(cols(g16, GROUP * HEAD_SIZE), grec, a_ss.at[3], a_rs.at[3]),
    ]
    weights = [(wo_ref, bufo), (wg_ref, bufg), (wu_ref, bufu), (wd_ref, bufd)]
    twin = dev(x, y, c, zl, zh)

    def swap(i):
        src, buf = weights[i]
        return src, buf.at[x, y, zh], w_ss.at[i], w_rs.at[i], twin

    def swap_start(first, last):
        for i in range(first, last):
            s, t, a, b, dest = swap(i)
            pl.when(home)(lambda s=s, t=t, b=b: pltpu.make_async_copy(s, t, b).start())
            pl.when(jnp.logical_not(home))(lambda s=s, t=t, a=a, b=b, dest=dest: remote(s, t, a, b, dest).start())

    def swap_wait(i):
        own = weights[i][1].at[x, y, c]
        remote(own, own, w_ss.at[i], w_rs.at[i], other).wait_recv()

    swap_start(0, 1)
    send_all(moves[0])
    send_all(moves[1])
    swap_start(1, 4)
    send_all(moves[2])
    send_all(moves[3])

    def close(*makes):
        for m in moves + list(makes):
            wait_all_sent(m)
        for i in range(4):
            s, t, a, b, dest = swap(i)
            pl.when(jnp.logical_not(home))(lambda s=s, t=t, a=a, b=b, dest=dest: remote(s, t, a, b, dest).wait_send())
        for cp in sent:
            cp.wait_send()

    sent = []

    def gather(buf, idx, x_first, at=(), halves=None, theirs_too=True):
        rx = dict(n=NX, me=x, to=xto, ss=x_ss.at[idx], rs=x_rs.at[idx], log=sent)
        ry = dict(n=NY, me=y, to=yto, ss=y_ss.at[idx], rs=y_rs.at[idx], log=sent)
        if x_first:
            one = Direct(lambda i: buf.at[(i, y, c) + at], **rx)
            two = Ring(lambda i: buf.at[(slice(None), i, c) + at], lambda i, w: buf.at[(pl.ds(w * 2, 2), i, c) + at], **ry)
        else:
            one = Ring(lambda i: buf.at[(x, i, c) + at], lambda i, w: buf.at[(x, i, c) + halves(w)], **ry)
            two = Ring(lambda i: buf.at[(i, slice(None), c) + at], lambda i, w: buf.at[(i, pl.ds(w * 4, 4), c) + at], **rx)

        def give(j, t):
            cp = remote(two.get(j), two.get(j), c_ss.at[idx, t], c_rs.at[idx, t], other)
            cp.start()
            sent.append(cp)

        one.start()
        yield
        if not x_first:
            for t in range(1, one.n // 2):
                one.step(t)
                yield
        one.finish()
        two.start()
        give(two.me, 0)
        yield
        for t in range(1, two.n // 2):
            two.step(t)
            give(two.pos(-t), 2 * t - 1)
            give(two.pos(t), 2 * t)
            yield
        two.finish()
        give(two.pos(two.n // 2), two.n - 1)
        yield
        if theirs_too:
            for t in range(two.n):
                theirs(buf, idx, x_first, t, at)
        yield

    def place(n, t):
        if t == n - 1:
            return n // 2
        return -((t + 1) // 2) if t % 2 else t // 2

    def spot(x_first, t):
        if x_first:
            return lax.rem(y + NY + place(NY, t), NY)
        return lax.rem(x + NX + place(NX, t), NX)

    def theirs(buf, idx, x_first, t, at):
        j = spot(x_first, t)
        ref = buf.at[((slice(None), j) if x_first else (j, slice(None))) + (1 - c,) + at]
        remote(ref, ref, c_ss.at[idx, t], c_rs.at[idx, t], other).wait_recv()

    def compact(rec, i):
        for s in range(8):
            cmp_buf[TOK * s:TOK * (s + 1), :] = rec[s].astype(F32)[:TOK]
        bufk[x, y, c, i] = cmp_buf[...].astype(BF16)

    every = slice(None)
    k_at = [(every, pl.ds(0, 48)), (every, pl.ds(48, 48))]
    ka = gather(bufk, 0, True, k_at[0], theirs_too=False)
    kb = gather(bufk, 1, False, k_at[1], lambda w: (pl.ds(w, 1), pl.ds(48, 48)), theirs_too=False)
    oa = gather(bufo, 2, True, (pl.ds(0, 16),))
    ob = gather(bufo, 3, False, (pl.ds(16, 16),), lambda w: (pl.ds(16, 16), pl.ds(w * 256, 256)))
    def halved(buf, idx, x_first):
        split = lambda lo: (lambda w: (pl.ds(lo, 16), pl.ds(w * 384, 384)))
        return [gather(buf, idx + i, x_first, (pl.ds(16 * i, 16),), split(16 * i)) for i in (0, 1)]

    g1, g2 = halved(bufg, 4, False)
    u1, u2 = halved(bufu, 6, True)
    d1, d2 = halved(bufd, 8, False)

    def go_on(*gens):
        for gen in gens:
            next(gen, None)

    power = math.log2(math.e) / math.sqrt(HEAD_SIZE)
    ones = jnp.ones((CHUNK, HEAD_SIZE), BF16)

    def attend(x_first, *arrivals):
        keys, vals, pos = [], [], []
        for t in arrivals:
            theirs(bufk, 0 if x_first else 1, x_first, t, k_at[0 if x_first else 1])
        for t in arrivals:
            j = spot(x_first, t)
            if x_first:
                keys.append(bufk[:, j, :, 0, 0:48].reshape(CHUNK // 2, HEAD_SIZE))
                vals.append(bufk[:, j, :, 1, 0:48].reshape(CHUNK // 2, HEAD_SIZE))
                pos.append(posa_ref[j])
            else:
                keys.append(bufk[j, :, :, 0, 48:96].reshape(CHUNK, HEAD_SIZE))
                vals.append(bufk[j, :, :, 1, 48:96].reshape(CHUNK, HEAD_SIZE))
                pos.append(posb_ref[j])
        join = lambda parts, axis: parts[0] if len(parts) == 1 else jnp.concatenate(parts, axis)
        keys, vals = join(keys, 0), jnp.concatenate([join(vals, 0), ones], 1)
        visible = join(pos, 1) <= tq_ref[...]
        for g in range(GROUP):
            q = qrec[:, :, g * HEAD_SIZE:(g + 1) * HEAD_SIZE].reshape(8 * PAD, HEAD_SIZE)
            s = lax.dot_general(q, keys, (((1,), (1,)), ((), ())), preferred_element_type=F32)
            s = jnp.where(visible, s, NEG)
            old = m_sc[g]
            new = jnp.maximum(old, jnp.broadcast_to(jnp.max(s, axis=1, keepdims=True), old.shape))
            p = jnp.exp2((s - jnp.concatenate([new] * (CHUNK // HEAD_SIZE), 1)) * power)
            f = jnp.exp2((old - new) * power)
            o = jnp.dot(p.astype(BF16), vals, preferred_element_type=F32)
            l_sc[g] = l_sc[g] * f + o[:, HEAD_SIZE:]
            acc[g] = acc[g] * f + o[:, :HEAD_SIZE]
            m_sc[g] = new

    swap_wait(0)
    go_on(oa, ob)
    wait_all_recv(krec, a_ss.at[0], a_rs.at[0])
    compact(krec, 0)
    wait_all_recv(vrec, a_ss.at[1], a_rs.at[1])
    compact(vrec, 1)
    go_on(kb, ka)
    m_sc[...] = jnp.full_like(m_sc, NEG)
    l_sc[...] = jnp.zeros_like(l_sc)
    acc[...] = jnp.zeros_like(acc)
    swap_wait(1)
    go_on(g1, g2)
    go_on(ob, kb, ka, oa)
    go_on(g1, g2)
    swap_wait(2)
    swap_wait(3)
    go_on(u1, u2)
    go_on(ob, kb, ka)
    go_on(g1, g2, d1)
    go_on(ob, kb, oa, ka)
    go_on(g1, g2, d1)
    go_on(kb, ob, g1)
    wait_all_recv(qrec, a_ss.at[2], a_rs.at[2])
    wait_all_recv(grec, a_ss.at[3], a_rs.at[3])
    attend(True, 1, 2)
    go_on(ka, oa, d1, d2)
    attend(False, 0)
    go_on(kb, ob, g2)
    go_on(u1)
    attend(True, 3, 4)
    go_on(d1, d2)
    go_on(ka, oa)
    go_on(g1)
    attend(True, 5, 6)
    go_on(kb, ob)
    go_on(d1, u2)
    attend(False, 1)
    go_on(oa, d2, u1)
    attend(False, 2)
    attend(True, 0, 7)
    go_on(g1, g2, d2)
    go_on(u1, u2)
    attend(False, 3)
    go_on(oa, ob)
    for g in range(GROUP):
        gate = grec[:, :, g * HEAD_SIZE:(g + 1) * HEAD_SIZE].reshape(8 * PAD, HEAD_SIZE).astype(F32)
        gated[:, g * HEAD_SIZE:(g + 1) * HEAD_SIZE] = (acc[g] / l_sc[g] * jax.nn.sigmoid(gate)).astype(BF16)

    NT = (((1,), (1,)), ((), ()))

    def collect(i, out, into, ss, rs):
        at = pl.ds(i * 384, 384)

        def make(d):
            dest, slot = in_peer(d)
            u = zl * 2 + zh
            return out.at[slot, :, at], into.at[u, :, at], ss.at[i, d], rs.at[i, u], dest
        return make

    def project(lhs, buf, width, out, into, ss, rs):
        makes = []
        for i in range(NX):
            part = lax.dot_general(lhs, buf[i].reshape(512, width), NT, preferred_element_type=F32)
            out[:, :, i * 384:(i + 1) * 384] = pack(part.reshape(8, PAD, 512)).astype(BF16)
            makes.append(collect(i, out, into, ss, rs))
            send_all(makes[-1])
        return makes

    def total(i, into, ss, rs):
        at = slice(i * 384, (i + 1) * 384)
        for u in range(8):
            ref = into.at[u, :, pl.ds(i * 384, 384)]
            remote(ref, ref, ss.at[i, u], rs.at[i, u], other).wait_recv()
        t = into[0, :, at].astype(F32)
        for u in range(1, 8):
            t = t + into[u, :, at].astype(F32)
        return unpack(t[None])[0]

    go_on(d2, d1)
    parts = project(gated[...], bufo, 512, pbuf, rbuf, r_ss, r_rs)
    go_on(u1, u2, g2, d2, u1, u2)
    square = jnp.zeros((PAD, 1), F32)
    for i in range(NX):
        at = slice(i * 512, (i + 1) * 512)
        h = (hid[:, at].astype(F32) + total(i, rbuf, r_ss, r_rs)).astype(BF16)
        hid[:, at] = h
        h = h.astype(F32)
        square += jnp.sum(h * h, axis=-1, keepdims=True)
    inv = lax.rsqrt(square * (1.0 / D) + 1e-06)
    for i in range(NX):
        at = slice(i * 512, (i + 1) * 512)
        nrm[:, i * 384:(i + 1) * 384] = pack((hid[:, at].astype(F32) * inv * gain_ref[:, at])[None])[0].astype(BF16)
    normed = spread(lambda head: nrm, nbuf, n_ss, n_rs)
    send_all(normed)
    go_on(u2, d1, d2)
    wait_all_recv(nbuf, n_ss, n_rs)
    for i in range(NX):
        at = slice(i * 512, (i + 1) * 512)
        rows[:, at] = unpack(nbuf[:, :, i * 384:(i + 1) * 384].astype(F32)).reshape(8 * PAD, 512).astype(BF16)
    go_on(g1, g2, u1, u2)
    for n in range(FFC // 256):
        at = slice(n * 256, (n + 1) * 256)
        gate_sum = jnp.zeros((8 * PAD, 256), F32)
        up_sum = jnp.zeros((8 * PAD, 256), F32)
        for i in range(NX):
            r = rows[:, i * 512:(i + 1) * 512]
            gate_sum += jnp.dot(r, bufg[i, :, :, :, at].reshape(512, 256), preferred_element_type=F32)
            up_sum += jnp.dot(r, bufu[i, :, :, :, at].reshape(512, 256), preferred_element_type=F32)
        act[:, at] = (jax.nn.silu(gate_sum) * up_sum).astype(BF16)
    go_on(d1, d2)
    parts += project(act[...], bufd, FFC, sbuf, fbuf, f_ss, f_rs)
    for i in range(NX):
        at = slice(i * 512, (i + 1) * 512)
        out_ref[:, at] = (hid[:, at].astype(F32) + total(i, fbuf, f_ss, f_rs))[:TOK].astype(BF16)
    close(normed, *parts)


def per_device(
    residual, query_projection, key_projection, value_projection, gate_proj, positions, prefix_len,
    out_weight, norm_gain, gate_weight, up_weight, down_weight,
):
    blk, uly = lax.axis_index("blk"), lax.axis_index("uly")
    first = (blk // 2 * 2 + uly % 2) * 96
    mine = lax.dynamic_slice_in_dim(positions, first, 96).reshape(8, TOK)
    tq = jnp.maximum(jnp.pad(mine, ((0, 0), (0, PAD - TOK))), prefix_len[0] - 1).reshape(8 * PAD, 1)
    pos = positions.reshape(NX, NY, 2, 2, 48)
    posa = pos[:, :, :, 0].transpose(1, 0, 2, 3).reshape(NY, 1, CHUNK // 2)
    posb = pos[:, :, :, 1].reshape(NX, 1, CHUNK)
    vm = pl.BlockSpec(memory_space=pltpu.VMEM)
    dma = pltpu.SemaphoreType.DMA
    half = lambda r, w: pltpu.VMEM((NX, NY, 2, r, w), BF16)
    return pl.pallas_call(
        kernel,
        out_shape=jax.ShapeDtypeStruct((TOK, D), BF16),
        in_specs=[vm] * 13,
        out_specs=vm,
        scratch_shapes=[
            pltpu.VMEM((PAD, 4096), BF16),
            pltpu.VMEM((PAD, 1024), BF16),
            pltpu.VMEM((PAD, 1024), BF16),
            pltpu.VMEM((PAD, 4096), BF16),
            pltpu.VMEM((8, PAD, 128), BF16),
            pltpu.VMEM((8, PAD, 128), BF16),
            pltpu.VMEM((8, PAD, 512), BF16),
            pltpu.VMEM((8, PAD, 512), BF16),
            pltpu.VMEM((96, 128), F32),
            pltpu.VMEM((NX, NY, 2, 2, 96, 128), BF16), half(32, 512), half(32, FFC), half(32, FFC), half(32, FFC),
            pltpu.VMEM((GROUP, 8 * PAD, HEAD_SIZE), F32),
            pltpu.VMEM((GROUP, 8 * PAD, HEAD_SIZE), F32),
            pltpu.VMEM((GROUP, 8 * PAD, HEAD_SIZE), F32),
            pltpu.VMEM((8 * PAD, GROUP * HEAD_SIZE), BF16),
            pltpu.VMEM((8, PAD, 1536), BF16),
            pltpu.VMEM((8, PAD, 1536), BF16),
            pltpu.VMEM((8, PAD, 1536), BF16),
            pltpu.VMEM((8, PAD, 1536), BF16),
            pltpu.VMEM((PAD, D), BF16),
            pltpu.VMEM((PAD, 1536), BF16),
            pltpu.VMEM((8, PAD, 1536), BF16),
            pltpu.VMEM((8 * PAD, D), BF16),
            pltpu.VMEM((8 * PAD, FFC), BF16),
            dma((4, 8)), dma((4, 8)),
            dma((4,)), dma((4,)),
            dma((10, 2, 2)), dma((10, 2, 2)),
            dma((10, 2, 4)), dma((10, 2, 4)),
            dma((10, 8)), dma((10, 8)),
            dma((4, 8)), dma((4, 8)),
            dma((8,)), dma((8,)),
            dma((4, 8)), dma((4, 8)),
        ],
        compiler_params=pltpu.CompilerParams(
            collective_id=0, has_side_effects=True, vmem_limit_bytes=60 * 2**20
        ),
        name="layer",
    )(
        query_projection, key_projection, value_projection, gate_proj, residual, tq, posa, posb,
        norm_gain.reshape(1, D), out_weight.T, gate_weight, up_weight, down_weight.T,
    )


def solution(mesh):
    return jax.shard_map(
        per_device,
        mesh=mesh,
        in_specs=(
            P(("blk", "uly"), None),
            P(("blk", "uly"), None),
            P(("blk", "uly"), None),
            P(("blk", "uly"), None),
            P(("blk", "uly"), None),
            P(),
            P(),
            P("uly", "blk"),
            P(),
            P("blk", "uly"),
            P("blk", "uly"),
            P("uly", "blk"),
        ),
        out_specs=P(("blk", "uly"), None),
        check_vma=False,
    )
```

```python
import functools
import math

import jax
import jax.numpy as jnp
from jax import lax
from jax.experimental import pallas as pl
from jax.experimental.pallas import tpu as pltpu
from jax.sharding import PartitionSpec as P

MESH = pl.DeviceIdType.MESH
HEAD_SIZE = 128
GROUP = 4
NX, NY = 4, 8
TOK = 12
PAD = 16
D = 2048
FFC = 768
CHUNK = 768
F32 = jnp.float32
BF16 = jnp.bfloat16
NEG = -1e30


def remote(src, dst, ss, rs, dest):
    return pltpu.make_async_remote_copy(
        src_ref=src, dst_ref=dst, send_sem=ss, recv_sem=rs, device_id=dest, device_id_type=MESH
    )


class Ring:
    def __init__(self, get, half, me, n, to, ss, rs, log):
        self.get, self.half, self.me, self.n, self.to, self.ss, self.rs = get, half, me, n, to, ss, rs
        self.sent = log

    def pos(self, d):
        return lax.rem(self.me + (d + self.n), self.n)

    def send(self, ref, way, t):
        step = 1 if way == 0 else -1
        cp = remote(ref, ref, self.ss.at[way, t], self.rs.at[way, t], self.to(self.pos(step)))
        cp.start()
        self.sent.append(cp)

    def wait(self, ref, way, t):
        remote(ref, ref, self.ss.at[way, t], self.rs.at[way, t], self.to(self.pos(1))).wait_recv()

    def start(self):
        own = self.get(self.me)
        self.send(own, 0, 0)
        self.send(own, 1, 0)

    def step(self, t):
        h = self.n // 2
        for way in (0, 1):
            j = self.pos(-t if way == 0 else t)
            self.wait(self.get(j), way, t - 1)
            self.send(self.get(j) if t < h - 1 else self.half(j, way), way, t)

    def finish(self):
        h = self.n // 2
        j = self.pos(h)
        for way in (0, 1):
            self.wait(self.half(j, way), way, h - 1)


class Direct:
    def __init__(self, get, me, n, to, ss, rs, log):
        self.get, self.me, self.n, self.to, self.ss, self.rs, self.sent = get, me, n, to, ss, rs, log

    def pos(self, d):
        return lax.rem(self.me + d, self.n)

    def start(self):
        own = self.get(self.me)
        for d in range(1, self.n):
            cp = remote(own, own, self.ss.at[d // 2, d % 2], self.rs.at[d // 2, d % 2], self.to(self.pos(d)))
            cp.start()
            self.sent.append(cp)

    def finish(self):
        for d in range(1, self.n):
            ref = self.get(self.pos(self.n - d))
            remote(ref, ref, self.ss.at[d // 2, d % 2], self.rs.at[d // 2, d % 2], self.to(self.pos(1))).wait_recv()


def pack(v):
    lo, hi = v[:, :8], v[:, 8:]
    turn = lambda t: jnp.concatenate([t[:, 4:], t[:, :4]], axis=1)
    extra = jnp.concatenate([turn(lo[..., 384:]), lo[..., 384:], turn(hi[..., 384:])], axis=2)
    row = lax.broadcasted_iota(jnp.int32, extra.shape, 1)
    return jnp.concatenate([lo[..., :384], jnp.where(row < 4, hi[..., :384], extra)], axis=1)


def unpack(v):
    lo, hi = v[:, :8], v[:, 8:]
    turn = lambda t: jnp.concatenate([t[:, 4:], t[:, :4]], axis=1)
    a, b, d = hi[..., :128], hi[..., 128:256], hi[..., 256:]
    row = lax.broadcasted_iota(jnp.int32, a.shape, 1)
    last = jnp.concatenate([jnp.where(row < 4, turn(a), b), turn(d)], axis=1)
    return jnp.concatenate([v, last], axis=2)


def kernel(
    q_ref, k_ref, v_ref, g_ref, res_ref, tq_ref, posk_ref, gain_ref, wo_ref, wg_ref, wu_ref, wd_ref,
    out_ref,
    q16, k16, v16, g16, krec, vrec, qrec, grec, cmp_buf,
    bufk, bufv, bufo, bufg, bufu, bufd,
    m_sc, l_sc, acc, gated, pbuf, rbuf, sbuf, fbuf, hid, nrm, nbuf, rows, act,
    a_ss, a_rs, w_ss, w_rs, x_ss, x_rs, y_ss, y_rs, c_ss, c_rs, r_ss, r_rs, n_ss, n_rs, f_ss, f_rs,
):
    blk, uly = lax.axis_index("blk"), lax.axis_index("uly")
    x, y, zh = lax.div(blk, 16), lax.rem(lax.div(blk, 2), 8), lax.rem(blk, 2)
    zl, c = lax.div(uly, 2), lax.rem(uly, 2)
    z = zh * 4 + zl

    def dev(x_, y_, zh_, zl_, c_):
        return ((x_ * NY + y_) * 2 + zh_, zl_ * 2 + c_)

    home = zh == c


    def out_peer(d):
        z2 = lax.rem(z + d, 8)
        zh2, zl2 = lax.div(z2, 4), lax.rem(z2, 4)
        return dev(x, y, zh2, zl2, zh), zl2 * 2 + zh2

    def in_peer(d):
        s = lax.rem(uly + d, 8)
        return dev(x, y, c, lax.div(s, 2), lax.rem(s, 2)), s

    other = dev(x, y, zh, zl, 1 - c)
    xto = lambda p: dev(p, y, zh, zl, c)
    yto = lambda p: dev(x, p, zh, zl, c)

    barrier = pltpu.get_barrier_semaphore()

    def greet(dest):
        pl.semaphore_signal(barrier, inc=1, device_id=dest, device_id_type=MESH)

    for d in range(1, NX):
        greet(xto(lax.rem(x + d, NX)))
    for d in (1, NY - 1):
        greet(yto(lax.rem(y + d, NY)))
    greet(other)
    for d in range(8):
        def both(d=d):
            greet(out_peer(d)[0])
            greet(in_peer(d)[0])
        if d == 0:
            pl.when(jnp.logical_not(home))(both)
        else:
            both()
    q16[0:TOK, :] = q_ref[...]
    k16[0:TOK, :] = k_ref[...]
    v16[0:TOK, :] = v_ref[...]
    g16[0:TOK, :] = g_ref[...]
    hid[0:TOK, :] = res_ref[...]
    pl.when(home)(lambda: pl.semaphore_wait(barrier, 20))
    pl.when(jnp.logical_not(home))(lambda: pl.semaphore_wait(barrier, 22))

    order = (4, 3, 5, 2, 6, 1, 7, 0)

    def spread(src, dst, ss, rs):
        def make(d):
            dest, head = out_peer(d)
            return src(head), dst.at[uly], ss.at[d], rs.at[uly], dest
        return make

    def send_all(make):
        for d in order:
            s, t, a, b, dest = make(d)
            if d == 0:
                pl.when(home)(lambda s=s, t=t, b=b: pltpu.make_async_copy(s, t, b).start())
                pl.when(jnp.logical_not(home))(lambda s=s, t=t, a=a, b=b, dest=dest: remote(s, t, a, b, dest).start())
            else:
                remote(s, t, a, b, dest).start()

    def wait_all_sent(make):
        for d in order:
            s, t, a, b, dest = make(d)
            if d == 0:
                pl.when(jnp.logical_not(home))(lambda s=s, t=t, a=a, b=b, dest=dest: remote(s, t, a, b, dest).wait_send())
            else:
                remote(s, t, a, b, dest).wait_send()

    def wait_all_recv(dst, ss, rs):
        for i in range(8):
            remote(dst.at[i], dst.at[i], ss.at[i], rs.at[i], other).wait_recv()

    def cols(ref, width):
        return lambda head: ref.at[:, pl.ds(pl.multiple_of(head * width, 128), width)]

    moves = [
        spread(cols(k16, HEAD_SIZE), krec, a_ss.at[0], a_rs.at[0]),
        spread(cols(v16, HEAD_SIZE), vrec, a_ss.at[1], a_rs.at[1]),
        spread(cols(q16, GROUP * HEAD_SIZE), qrec, a_ss.at[2], a_rs.at[2]),
        spread(cols(g16, GROUP * HEAD_SIZE), grec, a_ss.at[3], a_rs.at[3]),
    ]
    send_all(moves[0])
    send_all(moves[1])

    weights = [(wo_ref, bufo), (wg_ref, bufg), (wu_ref, bufu), (wd_ref, bufd)]
    twin = dev(x, y, c, zl, zh)

    def swap(i):
        src, buf = weights[i]
        return src, buf.at[x, y, zh], w_ss.at[i], w_rs.at[i], twin

    def swap_start():
        for i in range(4):
            s, t, a, b, dest = swap(i)
            pl.when(home)(lambda s=s, t=t, b=b: pltpu.make_async_copy(s, t, b).start())
            pl.when(jnp.logical_not(home))(lambda s=s, t=t, a=a, b=b, dest=dest: remote(s, t, a, b, dest).start())

    def swap_wait(i):
        own = weights[i][1].at[x, y, c]
        remote(own, own, w_ss.at[i], w_rs.at[i], other).wait_recv()

    swap_start()
    send_all(moves[2])
    send_all(moves[3])

    def close(*makes):
        for m in moves + list(makes):
            wait_all_sent(m)
        for i in range(4):
            s, t, a, b, dest = swap(i)
            pl.when(jnp.logical_not(home))(lambda s=s, t=t, a=a, b=b, dest=dest: remote(s, t, a, b, dest).wait_send())
        for cp in sent:
            cp.wait_send()

    sent = []

    def gather(buf, idx, x_first, rows, theirs_too=True):
        rx = dict(n=NX, me=x, to=xto, ss=x_ss.at[idx], rs=x_rs.at[idx], log=sent)
        ry = dict(n=NY, me=y, to=yto, ss=y_ss.at[idx], rs=y_rs.at[idx], log=sent)
        hr = rows // 2
        if x_first:
            one = Direct(lambda i: buf.at[i, y, c], **rx)
            two = Ring(lambda i: buf.at[:, i, c], lambda i, w: buf.at[pl.ds(w * 2, 2), i, c], **ry)
        else:
            one = Ring(lambda i: buf.at[x, i, c], lambda i, w: buf.at[x, i, c, pl.ds(w * hr, hr)], **ry)
            two = Ring(lambda i: buf.at[i, :, c], lambda i, w: buf.at[i, pl.ds(w * 4, 4), c], **rx)

        def give(j, t):
            cp = remote(two.get(j), two.get(j), c_ss.at[idx, t], c_rs.at[idx, t], other)
            cp.start()
            sent.append(cp)

        one.start()
        yield
        if not x_first:
            for t in range(1, one.n // 2):
                one.step(t)
                yield
        one.finish()
        two.start()
        give(two.me, 0)
        yield
        for t in range(1, two.n // 2):
            two.step(t)
            give(two.pos(-t), 2 * t - 1)
            give(two.pos(t), 2 * t)
            yield
        two.finish()
        give(two.pos(two.n // 2), two.n - 1)
        yield
        if theirs_too:
            for t in range(two.n):
                theirs(buf, idx, x_first, t)
        yield

    def place(n, t):
        if t == n - 1:
            return n // 2
        return -((t + 1) // 2) if t % 2 else t // 2

    def theirs(buf, idx, x_first, t):
        if x_first:
            ref = buf.at[:, lax.rem(y + NY + place(NY, t), NY), 1 - c]
        else:
            ref = buf.at[lax.rem(x + NX + place(NX, t), NX), :, 1 - c]
        remote(ref, ref, c_ss.at[idx, t], c_rs.at[idx, t], other).wait_recv()

    def compact(rec, buf):
        for s in range(8):
            cmp_buf[TOK * s:TOK * (s + 1), :] = rec[s].astype(F32)[:TOK]
        buf[x, y, c] = cmp_buf[...].astype(BF16)

    gk = gather(bufk, 0, True, 96, False)
    gv = gather(bufv, 1, True, 96, False)
    go = gather(bufo, 2, False, 32)
    gg = gather(bufg, 3, False, 32)
    gu = gather(bufu, 4, True, 32)
    gd = gather(bufd, 5, False, 32)

    def go_on(*gens):
        for gen in gens:
            next(gen, None)

    power = math.log2(math.e) / math.sqrt(HEAD_SIZE)
    ones = jnp.ones((CHUNK, HEAD_SIZE), BF16)

    def attend(first, last):
        for t in range(first, last):
            theirs(bufk, 0, True, t)
            theirs(bufv, 1, True, t)

        def body(i, _):
            far = lax.div(i + 1, 2)
            j = lax.rem(y + NY + jnp.where(jnp.logical_and(lax.rem(i, 2) == 1, i < NY - 1), -far, far), NY)
            keys = bufk[:, j].reshape(CHUNK, HEAD_SIZE)
            vals = jnp.concatenate([bufv[:, j].reshape(CHUNK, HEAD_SIZE), ones], 1)
            visible = posk_ref[j] <= tq_ref[...]
            for g in range(GROUP):
                q = qrec[:, :, g * HEAD_SIZE:(g + 1) * HEAD_SIZE].reshape(8 * PAD, HEAD_SIZE)
                s = lax.dot_general(q, keys, (((1,), (1,)), ((), ())), preferred_element_type=F32)
                s = jnp.where(visible, s, NEG)
                old = m_sc[g]
                new = jnp.maximum(old, jnp.broadcast_to(jnp.max(s, axis=1, keepdims=True), old.shape))
                p = jnp.exp2((s - jnp.concatenate([new] * (CHUNK // HEAD_SIZE), 1)) * power)
                f = jnp.exp2((old - new) * power)
                o = jnp.dot(p.astype(BF16), vals, preferred_element_type=F32)
                l_sc[g] = l_sc[g] * f + o[:, HEAD_SIZE:]
                acc[g] = acc[g] * f + o[:, :HEAD_SIZE]
                m_sc[g] = new
            return 0

        lax.fori_loop(first, last, body, 0)

    wait_all_recv(krec, a_ss.at[0], a_rs.at[0])
    compact(krec, bufk)
    go_on(gk)
    wait_all_recv(vrec, a_ss.at[1], a_rs.at[1])
    compact(vrec, bufv)
    go_on(gv)
    m_sc[...] = jnp.full_like(m_sc, NEG)
    l_sc[...] = jnp.zeros_like(l_sc)
    acc[...] = jnp.zeros_like(acc)
    swap_wait(0)
    go_on(go)
    go_on(gk, gv)
    go_on(go)
    for i in range(1, 4):
        swap_wait(i)
    go_on(gu)
    go_on(gk, gv)
    go_on(go, gg)
    wait_all_recv(qrec, a_ss.at[2], a_rs.at[2])
    wait_all_recv(grec, a_ss.at[3], a_rs.at[3])
    attend(0, 1)
    go_on(gk, gv)
    go_on(go, gg)
    attend(1, 3)
    go_on(go)
    go_on(gk, gv)
    go_on(gg, gd)
    go_on(gu)
    attend(3, 5)
    go_on(gg, gd)
    go_on(go)
    attend(5, 7)
    go_on(gg)
    go_on(gk, gv)
    go_on(go, gd)
    attend(7, 8)
    go_on(gd)
    for g in range(GROUP):
        gate = grec[:, :, g * HEAD_SIZE:(g + 1) * HEAD_SIZE].reshape(8 * PAD, HEAD_SIZE).astype(F32)
        gated[:, g * HEAD_SIZE:(g + 1) * HEAD_SIZE] = (acc[g] / l_sc[g] * jax.nn.sigmoid(gate)).astype(BF16)
    go_on(go)

    NT = (((1,), (1,)), ((), ()))

    def collect(i, out, into, ss, rs):
        at = pl.ds(i * 384, 384)

        def make(d):
            dest, slot = in_peer(d)
            u = zl * 2 + zh
            return out.at[slot, :, at], into.at[u, :, at], ss.at[i, d], rs.at[i, u], dest
        return make

    def project(lhs, buf, width, out, into, ss, rs):
        makes = []
        for i in range(NX):
            part = lax.dot_general(lhs, buf[i].reshape(512, width), NT, preferred_element_type=F32)
            out[:, :, i * 384:(i + 1) * 384] = pack(part.reshape(8, PAD, 512)).astype(BF16)
            makes.append(collect(i, out, into, ss, rs))
            send_all(makes[-1])
        return makes

    def total(i, into, ss, rs):
        at = slice(i * 384, (i + 1) * 384)
        for u in range(8):
            ref = into.at[u, :, pl.ds(i * 384, 384)]
            remote(ref, ref, ss.at[i, u], rs.at[i, u], other).wait_recv()
        t = into[0, :, at].astype(F32)
        for u in range(1, 8):
            t = t + into[u, :, at].astype(F32)
        return unpack(t[None])[0]

    parts = project(gated[...], bufo, 512, pbuf, rbuf, r_ss, r_rs)
    between = [(gu, gg), (gd,), (), (gu,)]
    square = jnp.zeros((PAD, 1), F32)
    for i in range(NX):
        at = slice(i * 512, (i + 1) * 512)
        go_on(*between[i])
        h = (hid[:, at].astype(F32) + total(i, rbuf, r_ss, r_rs)).astype(BF16)
        hid[:, at] = h
        h = h.astype(F32)
        square += jnp.sum(h * h, axis=-1, keepdims=True)
    inv = lax.rsqrt(square * (1.0 / D) + 1e-06)
    for i in range(NX):
        at = slice(i * 512, (i + 1) * 512)
        nrm[:, i * 384:(i + 1) * 384] = pack((hid[:, at].astype(F32) * inv * gain_ref[:, at])[None])[0].astype(BF16)
    normed = spread(lambda head: nrm, nbuf, n_ss, n_rs)
    send_all(normed)
    go_on(gg)
    go_on(gu)
    go_on(gd)
    go_on(gu)
    wait_all_recv(nbuf, n_ss, n_rs)
    for i in range(NX):
        at = slice(i * 512, (i + 1) * 512)
        rows[:, at] = unpack(nbuf[:, :, i * 384:(i + 1) * 384].astype(F32)).reshape(8 * PAD, 512).astype(BF16)
    go_on(gg, gu)
    for n in range(FFC // 256):
        at = slice(n * 256, (n + 1) * 256)
        gate_sum = jnp.zeros((8 * PAD, 256), F32)
        up_sum = jnp.zeros((8 * PAD, 256), F32)
        for i in range(NX):
            r = rows[:, i * 512:(i + 1) * 512]
            gate_sum += jnp.dot(r, bufg[i, :, :, :, at].reshape(512, 256), preferred_element_type=F32)
            up_sum += jnp.dot(r, bufu[i, :, :, :, at].reshape(512, 256), preferred_element_type=F32)
        act[:, at] = (jax.nn.silu(gate_sum) * up_sum).astype(BF16)
    go_on(gd, gd)
    parts += project(act[...], bufd, FFC, sbuf, fbuf, f_ss, f_rs)
    for i in range(NX):
        at = slice(i * 512, (i + 1) * 512)
        out_ref[:, at] = (hid[:, at].astype(F32) + total(i, fbuf, f_ss, f_rs))[:TOK].astype(BF16)
    close(normed, *parts)


def per_device(
    residual, query_projection, key_projection, value_projection, gate_proj, positions, prefix_len,
    out_weight, norm_gain, gate_weight, up_weight, down_weight,
):
    blk, uly = lax.axis_index("blk"), lax.axis_index("uly")
    first = (blk // 2 * 2 + uly % 2) * 96
    mine = lax.dynamic_slice_in_dim(positions, first, 96).reshape(8, TOK)
    tq = jnp.maximum(jnp.pad(mine, ((0, 0), (0, PAD - TOK))), prefix_len[0] - 1).reshape(8 * PAD, 1)
    posk = positions.reshape(NX, NY, CHUNK // NX).transpose(1, 0, 2).reshape(NY, 1, CHUNK)
    vm = pl.BlockSpec(memory_space=pltpu.VMEM)
    dma = pltpu.SemaphoreType.DMA
    half = lambda r, w: pltpu.VMEM((NX, NY, 2, r, w), BF16)
    return pl.pallas_call(
        kernel,
        out_shape=jax.ShapeDtypeStruct((TOK, D), BF16),
        in_specs=[vm] * 12,
        out_specs=vm,
        scratch_shapes=[
            pltpu.VMEM((PAD, 4096), BF16),
            pltpu.VMEM((PAD, 1024), BF16),
            pltpu.VMEM((PAD, 1024), BF16),
            pltpu.VMEM((PAD, 4096), BF16),
            pltpu.VMEM((8, PAD, 128), BF16),
            pltpu.VMEM((8, PAD, 128), BF16),
            pltpu.VMEM((8, PAD, 512), BF16),
            pltpu.VMEM((8, PAD, 512), BF16),
            pltpu.VMEM((96, 128), F32),
            half(96, 128), half(96, 128), half(32, 512), half(32, FFC), half(32, FFC), half(32, FFC),
            pltpu.VMEM((GROUP, 8 * PAD, HEAD_SIZE), F32),
            pltpu.VMEM((GROUP, 8 * PAD, HEAD_SIZE), F32),
            pltpu.VMEM((GROUP, 8 * PAD, HEAD_SIZE), F32),
            pltpu.VMEM((8 * PAD, GROUP * HEAD_SIZE), BF16),
            pltpu.VMEM((8, PAD, 1536), BF16),
            pltpu.VMEM((8, PAD, 1536), BF16),
            pltpu.VMEM((8, PAD, 1536), BF16),
            pltpu.VMEM((8, PAD, 1536), BF16),
            pltpu.VMEM((PAD, D), BF16),
            pltpu.VMEM((PAD, 1536), BF16),
            pltpu.VMEM((8, PAD, 1536), BF16),
            pltpu.VMEM((8 * PAD, D), BF16),
            pltpu.VMEM((8 * PAD, FFC), BF16),
            dma((4, 8)), dma((4, 8)),
            dma((4,)), dma((4,)),
            dma((6, 2, 2)), dma((6, 2, 2)),
            dma((6, 2, 4)), dma((6, 2, 4)),
            dma((6, 8)), dma((6, 8)),
            dma((4, 8)), dma((4, 8)),
            dma((8,)), dma((8,)),
            dma((4, 8)), dma((4, 8)),
        ],
        compiler_params=pltpu.CompilerParams(
            collective_id=0, has_side_effects=True, vmem_limit_bytes=60 * 2**20
        ),
        name="layer",
    )(
        query_projection, key_projection, value_projection, gate_proj, residual, tq, posk,
        norm_gain.reshape(1, D), out_weight.T, gate_weight, up_weight, down_weight.T,
    )


def solution(mesh):
    return jax.shard_map(
        per_device,
        mesh=mesh,
        in_specs=(
            P(("blk", "uly"), None),
            P(("blk", "uly"), None),
            P(("blk", "uly"), None),
            P(("blk", "uly"), None),
            P(("blk", "uly"), None),
            P(),
            P(),
            P("uly", "blk"),
            P(),
            P("blk", "uly"),
            P("blk", "uly"),
            P("uly", "blk"),
        ),
        out_specs=P(("blk", "uly"), None),
        check_vma=False,
    )
```
